256 devices in a mesh: gx: 16 (over y_hi, z), gy: 16 (over x, y_lo, core).
Axes of the slice: x: 4, y: 4 (y_hi: 2, y_lo: 2; y = y_hi * 2 + y_lo), z: 8, core: 2. Of those that a mesh axis runs over, the one named last changes fastest.
Arguments:
- wavefield: bfloat16 [2, 1, 7168, 7168], P(None, None, 'gx', 'gy'), may hold values from -6 to 6
- slowness: float32 [7168, 7168], P('gx', 'gy'), may hold values from -4 to 4
- frequencies: float32 [1], replicated, may hold values from 1 to 4
- propagator: bfloat16 [3, 1, 2, 256, 256], replicated, may hold values from -0.25 to 0.25
- window_velocity_group: int32 [32, 32], replicated, may hold values from 0 to 2
- reach_list: int32 [32, 32, 5], replicated, may hold values from -1 to 1023, as said below
- coupling: float32 [32, 32, 5, 2], replicated, may hold values from -3 to 3
Outputs:
- migrated: bfloat16 [2, 1, 7168, 7168], P(None, None, 'gx', 'gy')
The draws below stay inside these ranges and needn't reach their ends.
Inputs may be any that keep to these rules, and one draw needn't show every extreme that they name: `reach_list`: slot 0 of window (x, y) holds the window itself, x * 32 + y. Every other slot holds -1 or one of the eight windows that touch (x, y) along x, y or a diagonal; the entries of one list are distinct apart from -1. Some windows have one live entry, some have 5.
All inputs are finite; a program needn't handle non-finite values.
Results may differ from the reference program's by a relative error of at most 0.01.
Values may be sent and summed in bfloat16 or wider, within the bound.
A program may use at most 64 MiB of HBM per device.

```python
import math
import jax
import jax.numpy as jnp
from jax import lax

WINDOW_CELLS = 256
OVER = 32
FREQUENCY_COUNT = 1
VELOCITY_GROUPS = 3
SLOTS = 5
WINDOWS_ALONG_X = 32
WINDOWS_ALONG_Y = 32
NX = 7168
NY = 7168


def draw_reach_list(key, part):
    base_key = jax.random.fold_in(key, 7)
    count_key, order_key = jax.random.split(base_key, 2)
    counts = jax.random.randint(count_key, (WINDOWS_ALONG_X, WINDOWS_ALONG_Y), 1, SLOTS + 1)
    counts = counts.at[0, 0].set(1).at[WINDOWS_ALONG_X - 1, WINDOWS_ALONG_Y - 1].set(SLOTS)
    scores = jax.random.randint(order_key, (WINDOWS_ALONG_X, WINDOWS_ALONG_Y, 8), 0, 1 << 20) * 8 + jnp.arange(8)
    ordering = jnp.argsort(scores, axis=-1)[..., :SLOTS - 1]
    offset_x = jnp.array([-1, -1, -1, 0, 0, 1, 1, 1], dtype=jnp.int32)
    offset_y = jnp.array([-1, 0, 1, -1, 1, -1, 0, 1], dtype=jnp.int32)
    neighbour_x = jnp.arange(WINDOWS_ALONG_X)[:, None, None] + offset_x[ordering]
    neighbour_y = jnp.arange(WINDOWS_ALONG_Y)[None, :, None] + offset_y[ordering]
    inside = (neighbour_x >= 0) & (neighbour_x < WINDOWS_ALONG_X) & (neighbour_y >= 0) & (neighbour_y < WINDOWS_ALONG_Y)
    wanted = (jnp.arange(1, SLOTS)[None, None, :] < counts[:, :, None]) & inside
    others = jnp.where(wanted, neighbour_x * WINDOWS_ALONG_Y + neighbour_y, -1)
    itself = (jnp.arange(WINDOWS_ALONG_X)[:, None] * WINDOWS_ALONG_Y + jnp.arange(WINDOWS_ALONG_Y)[None, :])[:, :, None]
    return jnp.concatenate([itself, others], axis=2).astype(jnp.int32)


def set_ends(entries, key, smallest, largest):
    shape = entries.shape
    index_at = [jax.random.randint(jax.random.fold_in(key, axis), (), 0, shape[axis]) for axis in range(len(shape))]
    entries = entries.at[tuple(index_at)].set(smallest)
    longest = shape.index(max(shape))
    index_at[longest] = (index_at[longest] + 1) % shape[longest]
    return entries.at[tuple(index_at)].set(largest)


def block_scale(rng, dims, shards, least, largest):
    def one(dim, parts):
        heights = jax.random.uniform(jax.random.fold_in(jax.random.fold_in(rng, 6), dim), (parts,), jnp.float32, least / len(shards), largest / len(shards))
        return jnp.repeat(jnp.exp(heights), dims[dim] // parts).reshape((-1,) + (1,) * (len(dims) - dim - 1))

    gain = one(*shards[0])
    for cut in shards[1:]:
        gain = gain * one(*cut)
    return gain


def gaussian(key, extent, scale, bound, cuts=(), kind=jnp.bfloat16):
    gain = block_scale(key, extent, cuts, -0.22, 0.18) if cuts else 1.0
    values = jax.random.normal(key, extent, jnp.float32) * scale * gain
    return jnp.minimum(jnp.maximum(values, -bound), bound).astype(kind)


def setup_inputs(seed: int = 0) -> dict:
    key_list = jax.random.split(jax.random.key(seed), 8)
    return {
        "wavefield": gaussian(key_list[0], (2, FREQUENCY_COUNT, NX, NY), 1.0, 6.0, ((2, 16), (3, 16))),
        "slowness": gaussian(key_list[1], (NX, NY), 0.6, 4.0, ((0, 16), (1, 16)), jnp.float32),
        "frequencies": jnp.clip(jax.random.uniform(key_list[2], (FREQUENCY_COUNT,), jnp.float32, 1.0, 4.0), 1.0, 4.0),
        "propagator": gaussian(key_list[3], (VELOCITY_GROUPS, FREQUENCY_COUNT, 2, WINDOW_CELLS, WINDOW_CELLS), (2 * WINDOW_CELLS) ** -0.5, 0.25),
        "window_velocity_group": set_ends(jax.random.randint(key_list[4], (WINDOWS_ALONG_X, WINDOWS_ALONG_Y), 0, VELOCITY_GROUPS), jax.random.fold_in(key_list[4], 1), 0, VELOCITY_GROUPS - 1).astype(jnp.int32),
        "reach_list": draw_reach_list(jax.random.fold_in(key_list[7], 71), 0),
        "coupling": gaussian(key_list[6], (WINDOWS_ALONG_X, WINDOWS_ALONG_Y, SLOTS, 2), 0.5, 3.0, (), jnp.float32),
    }


def cosine_table(length):
    points = jnp.arange(length, dtype=jnp.float32) + 0.5
    return jnp.sqrt(2.0 / length) * jnp.cos(math.pi / length * points[:, None] * points[None, :])

def bell_curve(length, margin):
    points = jnp.arange(length, dtype=jnp.float32)
    rising = jnp.sin(0.5 * math.pi * (points + 0.5) / margin)
    falling = jnp.cos(0.5 * math.pi * (points - (length - margin) + 0.5) / margin)
    return jnp.where(points < margin, rising, jnp.where(points >= length - margin, falling, 1.0))

def rounded(values):
    return lax.optimization_barrier(values.astype(jnp.bfloat16))

def complex_apply(spec, matrix_real, matrix_imag, data_real, data_imag):

    def contract(left, right):
        return jnp.einsum(spec, left.astype(jnp.float32), right.astype(jnp.float32))
    real_part = contract(matrix_real, data_real) - contract(matrix_imag, data_imag)
    imag_part = contract(matrix_real, data_imag) + contract(matrix_imag, data_real)
    return rounded(jnp.stack([real_part, imag_part]))

def one_frequency(wave_slice, prop_slice, angular, slowness, window_velocity_group, reach_list, coupling):
    half_rim = OVER // 2
    stride = WINDOW_CELLS - OVER
    cosines = rounded(cosine_table(WINDOW_CELLS)).astype(jnp.float32)
    bell_values = bell_curve(WINDOW_CELLS, OVER)
    padded = jnp.pad(wave_slice, ((0, 0), (half_rim, half_rim), (half_rim, half_rim)))
    row_cells = (jnp.arange(WINDOWS_ALONG_X) * stride)[:, None] + jnp.arange(WINDOW_CELLS)[None, :]
    col_cells = (jnp.arange(WINDOWS_ALONG_Y) * stride)[:, None] + jnp.arange(WINDOW_CELLS)[None, :]
    patches = padded[:, row_cells][:, :, :, col_cells]
    tapered = rounded(patches.astype(jnp.float32) * bell_values[None, None, :, None, None] * bell_values)
    first_pass = rounded(jnp.einsum('lb,pxayb->pxayl', cosines, tapered.astype(jnp.float32)))
    coefficients = rounded(jnp.einsum('ka,pxayl->pxkyl', cosines, first_pass.astype(jnp.float32)))
    chosen = prop_slice[window_velocity_group]
    swept_coefs = complex_apply('xymk,xkyl->xmyl', chosen[:, :, 0], chosen[:, :, 1], coefficients[0], coefficients[1])
    by_window = jnp.transpose(swept_coefs, (0, 1, 3, 2, 4)).reshape(2, WINDOWS_ALONG_X * WINDOWS_ALONG_Y, WINDOW_CELLS, WINDOW_CELLS).astype(jnp.float32)
    is_live = reach_list >= 0
    safe_index = jnp.where(is_live, reach_list, 0)
    scale_real = jnp.where(is_live, coupling[..., 0], 0.0)
    scale_imag = jnp.where(is_live, coupling[..., 1], 0.0)
    mixed_real = jnp.zeros((WINDOWS_ALONG_X, WINDOWS_ALONG_Y, WINDOW_CELLS, WINDOW_CELLS), jnp.float32)
    mixed_imag = jnp.zeros((WINDOWS_ALONG_X, WINDOWS_ALONG_Y, WINDOW_CELLS, WINDOW_CELLS), jnp.float32)
    for slot_index in range(SLOTS):
        picked = by_window[:, safe_index[:, :, slot_index]]
        weight_real = scale_real[:, :, slot_index][:, :, None, None]
        weight_imag = scale_imag[:, :, slot_index][:, :, None, None]
        mixed_real = mixed_real + weight_real * picked[0] - weight_imag * picked[1]
        mixed_imag = mixed_imag + weight_real * picked[1] + weight_imag * picked[0]
    mixed_coefs = rounded(jnp.stack([mixed_real, mixed_imag]))
    propagated = complex_apply('xynl,xykl->xykn', chosen[:, :, 0], chosen[:, :, 1], mixed_coefs[0], mixed_coefs[1])
    second = rounded(jnp.einsum('lb,pxykl->pxykb', cosines, propagated.astype(jnp.float32)))
    pieces = jnp.einsum('ka,pxykb->pxayb', cosines, second.astype(jnp.float32))
    pieces = pieces * bell_values[None, None, :, None, None] * bell_values
    canvas = jnp.zeros((2, WINDOWS_ALONG_X * stride + OVER, WINDOWS_ALONG_Y * stride + OVER), jnp.float32)
    canvas = canvas.at[:, row_cells[:, :, None, None], col_cells[None, None, :, :]].add(pieces)
    summed = canvas[:, half_rim:half_rim + WINDOWS_ALONG_X * stride, half_rim:half_rim + WINDOWS_ALONG_Y * stride]
    phases = angular * slowness
    cos_phase = jnp.cos(phases)
    sin_phase = jnp.sin(phases)
    out_real = summed[0] * cos_phase - summed[1] * sin_phase
    out_imag = summed[0] * sin_phase + summed[1] * cos_phase
    return jnp.stack([out_real, out_imag]).astype(jnp.bfloat16)

def reference(wavefield, slowness, frequencies, propagator, window_velocity_group, reach_list, coupling):

    def per_frequency(inputs):
        wave_slice, prop_slice, angular = inputs
        return one_frequency(wave_slice, prop_slice, angular, slowness, window_velocity_group, reach_list, coupling)
    results = lax.map(per_frequency, (jnp.transpose(wavefield, (1, 0, 2, 3)), jnp.transpose(propagator, (1, 0, 2, 3, 4)), frequencies))
    return jnp.transpose(results, (1, 0, 2, 3))
```

```python
import functools

import jax
import jax.numpy as jnp
import numpy as np
from jax import lax
from jax.experimental import pallas as pl
from jax.experimental.pallas import tpu as pltpu
from jax.sharding import PartitionSpec as P

LENGTH = 256
OVER = 32
RIM = OVER // 2
STRIDE = LENGTH - OVER
TILE = 2 * STRIDE
WIDE = 2 * LENGTH
HALF = LENGTH // 2
CHUNK = 16
BF16 = jnp.bfloat16
F32 = jnp.float32


def tables():
    points = np.arange(LENGTH) + 0.5
    cosines = np.sqrt(2.0 / LENGTH) * np.cos(np.pi / LENGTH * points[:, None] * points[None, :])
    cosines = cosines.astype(np.float32).astype(jnp.bfloat16).astype(np.float64)
    cells = np.arange(LENGTH)
    rising = np.sin(0.5 * np.pi * (cells + 0.5) / OVER)
    falling = np.cos(0.5 * np.pi * (cells - STRIDE + 0.5) / OVER)
    bell = np.where(cells < OVER, rising, np.where(cells >= STRIDE, falling, 1.0))
    tapered = cosines * bell[None, :]
    across = np.zeros((WIDE, WIDE))
    for window in range(2):
        for cell in range(LENGTH):
            at = window * STRIDE + cell - RIM
            if at < 0:
                at = TILE + at + RIM
            elif at >= TILE:
                at = RIM + at
            across[at, window * LENGTH : (window + 1) * LENGTH] = tapered[:, cell]

    def low(array):
        return np.ascontiguousarray(array).astype(np.float32).astype(jnp.bfloat16)

    return low(across), low(across.T), low(tapered), low(tapered.T)


NEEDED = []
for _tx in (0, 1):
    for _ty in (0, 1):
        NEEDED += [(_tx, _ty, _dx, _dy) for _dx in (-1, 0, 1) for _dy in (-1, 0, 1)]
for _t in (0, 1):
    NEEDED += [(_t, -1, _dx, 1) for _dx in (-1, 0, 1)]
    NEEDED += [(_t, 2, _dx, -1) for _dx in (-1, 0, 1)]
    NEEDED += [(-1, _t, 1, _dy) for _dy in (-1, 0, 1)]
    NEEDED += [(2, _t, -1, _dy) for _dy in (-1, 0, 1)]
PLACE = {key: index for index, key in enumerate(NEEDED)}


def contract(left, right, left_dim, right_dim):
    return lax.dot_general(
        left, right, (((left_dim,), (right_dim,)), ((), ())), preferred_element_type=F32
    )


def selector(rows, columns, target):
    row = lax.broadcasted_iota(jnp.int32, (rows, columns), 0)
    column = lax.broadcasted_iota(jnp.int32, (rows, columns), 1)
    return jnp.where(column == target(row), 1.0, 0.0).astype(BF16)


def kernel(
    sizes,
    x_hbm,
    slow_hbm,
    freq,
    prop_hbm,
    group,
    reach,
    coup,
    a1_hbm,
    b1_hbm,
    a2_hbm,
    b2_hbm,
    out,
    xv,
    slow,
    prop,
    a1,
    b1,
    a2,
    b2,
    hs,
    hr,
    fp32,
    fp,
    cf,
    swa,
    swb,
    ra,
    rb,
    pa,
    pb,
    qa,
    qb,
    acc,
    mixed,
    pg,
    canvas,
    cosv,
    sinv,
    ors,
    orr,
    ocs,
    ocr,
    weights,
    local_sem,
    send_sem,
    recv_sem,
):
    size_x, size_y = sizes
    gx = lax.axis_index("gx")
    gy = lax.axis_index("gy")
    has = {
        ("gx", -1): gx > 0,
        ("gx", 1): gx < size_x - 1,
        ("gy", -1): gy > 0,
        ("gy", 1): gy < size_y - 1,
    }
    here = {"gx": gx, "gy": gy}

    loads = [
        pltpu.make_async_copy(source, target, local_sem.at[index])
        for index, (source, target) in enumerate(
            [
                (x_hbm.at[:, 0], xv),
                (a1_hbm, a1),
                (a2_hbm, a2),
                (prop_hbm.at[:, 0], prop),
                (slow_hbm, slow),
                (b1_hbm, b1),
                (b2_hbm, b2),
            ]
        )
    ]
    for load in loads:
        load.start()

    barrier = pltpu.get_barrier_semaphore()
    for (axis, step), there in has.items():

        @pl.when(there)
        def _(axis=axis, step=step):
            pl.semaphore_signal(
                barrier,
                inc=1,
                device_id={axis: here[axis] + step},
                device_id_type=pl.DeviceIdType.MESH,
            )

    def message(number, axis, step, source, target):
        slot = 2 * number + (step + 1) // 2
        return pltpu.make_async_remote_copy(
            src_ref=source,
            dst_ref=target,
            send_sem=send_sem.at[slot],
            recv_sem=recv_sem.at[slot],
            device_id={axis: here[axis] + step},
            device_id_type=pl.DeviceIdType.MESH,
        )

    def start(number, axis, ways):
        for step, (source, target) in ways.items():

            @pl.when(has[axis, step])
            def _(step=step, source=source, target=target):
                message(number, axis, step, source, target).start()

    def arrive(number, axis, ways):
        for step, (source, target) in ways.items():

            @pl.when(has[axis, -step])
            def _(step=step, source=source, target=target):
                message(number, axis, step, source, target).wait_recv()

    def drain(number, axis, ways):
        for step, (source, target) in ways.items():

            @pl.when(has[axis, step])
            def _(step=step, source=source, target=target):
                message(number, axis, step, source, target).wait_send()

    def clear_missing(axis, ways):
        for step, (_, target) in ways.items():

            @pl.when(jnp.logical_not(has[axis, -step]))
            def _(target=target):
                target[...] = jnp.zeros(target.shape, target.dtype)

    rim_ways = {-1: (hs.at[0], hr.at[1]), 1: (hs.at[1], hr.at[0])}
    row_ways = {
        -1: (fp.at[:, RIM : 2 * RIM], fp.at[:, TILE + RIM : TILE + OVER]),
        1: (fp.at[:, TILE : TILE + RIM], fp.at[:, 0:RIM]),
    }
    a_ways = {-1: (swa.at[0], ra.at[1]), 1: (swa.at[1], ra.at[0])}
    b_ways = {-1: (swb.at[0], rb.at[1]), 1: (swb.at[1], rb.at[0])}
    pa_ways = {-1: (pa.at[0], qa.at[1]), 1: (pa.at[1], qa.at[0])}
    pb_ways = {-1: (pb.at[0], qb.at[1]), 1: (pb.at[1], qb.at[0])}
    or_ways = {-1: (ors.at[0], orr.at[1]), 1: (ors.at[1], orr.at[0])}
    oc_ways = {-1: (ocs.at[0], ocr.at[1]), 1: (ocs.at[1], ocr.at[0])}

    pick = selector(OVER, TILE, lambda r: jnp.where(r < RIM, r, r + TILE - OVER))
    loads[0].wait()
    for part in range(2):
        rims = contract(pick, xv[part], 1, 1).astype(BF16)
        hs[0, part] = rims[:RIM]
        hs[1, part] = rims[RIM:]
    clear_missing("gy", rim_ways)
    clear_missing("gx", row_ways)
    clear_missing("gx", a_ways)
    clear_missing("gy", b_ways)
    clear_missing("gy", pa_ways)
    clear_missing("gx", pb_ways)
    clear_missing("gx", or_ways)
    clear_missing("gy", oc_ways)
    pl.semaphore_wait(barrier, sum(there.astype(jnp.int32) for there in has.values()))
    start(0, "gy", rim_ways)

    loads[1].wait()
    for part in range(2):
        fp32[part] = jnp.dot(xv[part], a1[:TILE], preferred_element_type=F32)
    arrive(0, "gy", rim_ways)
    for part in range(2):
        rims = jnp.concatenate([hr[0, part], hr[1, part]], axis=0)
        fp[part, RIM : TILE + RIM] = (
            fp32[part] + contract(rims, a1[TILE : TILE + OVER], 0, 0)
        ).astype(BF16)
    start(1, "gx", row_ways)

    total_x = 2 * size_x
    total_y = 2 * size_y
    for tx, ty in sorted({key[:2] for key in NEEDED}):
        at_x = 2 * gx + tx
        at_y = 2 * gy + ty
        near_x = jnp.clip(at_x, 0, total_x - 1)
        near_y = jnp.clip(at_y, 0, total_y - 1)
        slots = [
            (reach[s, near_x, near_y], coup[near_x, s, 0, near_y], coup[near_x, s, 1, near_y])
            for s in range(reach.shape[0])
        ]
        for key, place in PLACE.items():
            if key[:2] != (tx, ty):
                continue
            window = (at_x + key[2]) * total_y + at_y + key[3]
            window = jnp.where(at_x + key[2] < 0, -2, window)
            real = jnp.float32(0.0)
            imag = jnp.float32(0.0)
            for entry, entry_real, entry_imag in slots:
                same = entry == window
                real = jnp.where(same, entry_real, real)
                imag = jnp.where(same, entry_imag, imag)
            weights[2 * place] = real
            weights[2 * place + 1] = imag

    loads[2].wait()
    loads[3].wait()
    arrive(1, "gx", row_ways)
    for part in range(2):
        for wx in range(2):
            cf[part, wx] = jnp.dot(
                a2[...],
                fp[part, wx * STRIDE : wx * STRIDE + LENGTH],
                preferred_element_type=F32,
            ).astype(BF16)

    def group_of(wx, wy):
        return group[2 * gx + wx, 2 * gy + wy]

    def sweep(half, wx, wy):
        which = group_of(wx, wy)
        g_real = prop[which, 0, half * HALF : (half + 1) * HALF]
        g_imag = prop[which, 1, half * HALF : (half + 1) * HALF]
        c_real = cf[0, wx, :, wy * LENGTH : (wy + 1) * LENGTH]
        c_imag = cf[1, wx, :, wy * LENGTH : (wy + 1) * LENGTH]

        def dot(left, right):
            return jnp.dot(left, right, preferred_element_type=F32)

        real = dot(g_real, c_real) - dot(g_imag, c_imag)
        imag = dot(g_real, c_imag) + dot(g_imag, c_real)
        return real.astype(BF16), imag.astype(BF16)

    for wx in range(2):
        for wy in range(2):
            swa[wx, wy, 0], swa[wx, wy, 1] = sweep(0, wx, wy)
    start(2, "gx", a_ways)
    for wy in range(2):
        for wx in range(2):
            swb[wy, wx, 0], swb[wy, wx, 1] = sweep(1, wx, wy)
    start(3, "gy", b_ways)

    def source(half, x, y):
        if half == 0:
            if x in (0, 1):
                return swa.at[x, y]
            return ra.at[0 if x < 0 else 1, y]
        if y in (0, 1):
            return swb.at[y, x]
        return rb.at[0 if y < 0 else 1, x]

    def rows(chunk):
        return pl.ds(pl.multiple_of(chunk * CHUNK, CHUNK), CHUNK)

    def mix(half, sums, get, put):
        def body(chunk, carry):
            at = rows(chunk)
            held = {}

            def value(x, y):
                if (x, y) not in held:
                    ref = source(half, x, y)
                    held[x, y] = (ref[0, at, :].astype(F32), ref[1, at, :].astype(F32))
                return held[x, y]

            for (tx, ty), sources in sums:
                real, imag = get(tx, ty, at) if get is not None else (None, None)
                for sx, sy in sources:
                    place = PLACE[tx, ty, sx - tx, sy - ty]
                    w_real = weights[2 * place]
                    w_imag = weights[2 * place + 1]
                    v_real, v_imag = value(sx, sy)
                    add_real = w_real * v_real - w_imag * v_imag
                    add_imag = w_real * v_imag + w_imag * v_real
                    real = add_real if real is None else real + add_real
                    imag = add_imag if imag is None else imag + add_imag
                put(tx, ty, at, real, imag)
            return carry

        lax.fori_loop(0, HALF // CHUNK, body, 0)

    def acc_get(half):
        def get(tx, ty, at):
            return acc[half, tx, ty, 0, at, :], acc[half, tx, ty, 1, at, :]

        return get

    def acc_put(half):
        def put(tx, ty, at, real, imag):
            acc[half, tx, ty, 0, at, :] = real
            acc[half, tx, ty, 1, at, :] = imag

        return put

    inner = [(x, y) for x in (0, 1) for y in (0, 1)]
    for half in range(2):
        mix(half, [(target, inner) for target in inner], None, acc_put(half))

    loads[4].wait()

    def phase_rows(chunk, carry):
        at = rows(chunk)
        angle = freq[0] * slow[at, :]
        cosv[at, :] = jnp.cos(angle)
        sinv[at, :] = jnp.sin(angle)
        return carry

    lax.fori_loop(0, TILE // CHUNK, phase_rows, 0)

    def pa_put(tx, ty, at, real, imag):
        side = 0 if ty < 0 else 1
        pa[side, tx, 0, at, :] = real.astype(BF16)
        pa[side, tx, 1, at, :] = imag.astype(BF16)

    def pb_put(tx, ty, at, real, imag):
        side = 0 if tx < 0 else 1
        pb[side, ty, 0, at, :] = real.astype(BF16)
        pb[side, ty, 1, at, :] = imag.astype(BF16)

    arrive(2, "gx", a_ways)
    mix(
        0,
        [((t, -1), [(t + d, 0) for d in (-1, 0, 1)]) for t in (0, 1)]
        + [((t, 2), [(t + d, 1) for d in (-1, 0, 1)]) for t in (0, 1)],
        None,
        pa_put,
    )
    start(4, "gy", pa_ways)
    arrive(3, "gy", b_ways)
    mix(
        1,
        [((-1, t), [(0, t + d) for d in (-1, 0, 1)]) for t in (0, 1)]
        + [((2, t), [(1, t + d) for d in (-1, 0, 1)]) for t in (0, 1)],
        None,
        pb_put,
    )
    start(5, "gx", pb_ways)
    mix(
        0,
        [((0, y), [(-1, 0), (-1, 1)]) for y in (0, 1)] + [((1, y), [(2, 0), (2, 1)]) for y in (0, 1)],
        acc_get(0),
        acc_put(0),
    )
    mix(
        1,
        [((x, 0), [(0, -1), (1, -1)]) for x in (0, 1)] + [((x, 1), [(0, 2), (1, 2)]) for x in (0, 1)],
        acc_get(1),
        acc_put(1),
    )

    arrive(4, "gy", pa_ways)
    arrive(5, "gx", pb_ways)

    def join(chunk, carry):
        at = rows(chunk)
        below = pl.ds(pl.multiple_of(HALF + chunk * CHUNK, CHUNK), CHUNK)
        for tx, ty in inner:
            for part in range(2):
                mixed[tx, ty, part, at, :] = (
                    acc[0, tx, ty, part, at, :] + qa[ty, tx, part, at, :].astype(F32)
                ).astype(BF16)
                mixed[tx, ty, part, below, :] = (
                    acc[1, tx, ty, part, at, :] + qb[tx, ty, part, at, :].astype(F32)
                ).astype(BF16)
        return carry

    lax.fori_loop(0, HALF // CHUNK, join, 0)

    loads[5].wait()
    loads[6].wait()
    for wx in range(2):
        for wy in range(2):
            which = group_of(wx, wy)
            g_real = prop[which, 0]
            g_imag = prop[which, 1]
            m_real = mixed[wx, wy, 0]
            m_imag = mixed[wx, wy, 1]
            real = contract(m_real, g_real, 1, 1) - contract(m_imag, g_imag, 1, 1)
            imag = contract(m_imag, g_real, 1, 1) + contract(m_real, g_imag, 1, 1)
            pg[wx, 0, :, wy * LENGTH : (wy + 1) * LENGTH] = real.astype(BF16)
            pg[wx, 1, :, wy * LENGTH : (wy + 1) * LENGTH] = imag.astype(BF16)
    for part in range(2):
        pieces = []
        for wx in range(2):
            second = jnp.dot(pg[wx, part], b1[...], preferred_element_type=F32).astype(BF16)
            pieces.append(jnp.dot(b2[...], second, preferred_element_type=F32))
        canvas[part, 0:STRIDE] = pieces[0][:STRIDE]
        canvas[part, STRIDE:LENGTH] = pieces[0][STRIDE:] + pieces[1][:OVER]
        canvas[part, LENGTH : TILE + OVER] = pieces[1][OVER:]
    ors[0] = canvas[:, 0:RIM].astype(BF16)
    ors[1] = canvas[:, TILE + RIM : TILE + OVER].astype(BF16)
    start(6, "gx", or_ways)
    arrive(6, "gx", or_ways)
    canvas[:, RIM : 2 * RIM] = canvas[:, RIM : 2 * RIM] + orr[0].astype(F32)
    canvas[:, TILE : TILE + RIM] = canvas[:, TILE : TILE + RIM] + orr[1].astype(F32)
    own = slice(RIM, TILE + RIM)
    pick_rim = selector(OVER, 128, lambda r: r + 64)
    for part in range(2):
        rims = contract(pick_rim, canvas[part, own, 384:512].astype(BF16), 1, 1).astype(BF16)
        ocs[0, part] = rims[:RIM]
        ocs[1, part] = rims[RIM:]
    start(7, "gy", oc_ways)
    arrive(7, "gy", oc_ways)
    first = selector(RIM, 128, lambda r: r)
    last = selector(RIM, 128, lambda r: r + 48)
    for part in range(2):
        canvas[part, own, 0:128] = canvas[part, own, 0:128] + contract(ocr[0, part], first, 0, 0)
        canvas[part, own, 384:512] = canvas[part, own, 384:512] + contract(ocr[1, part], last, 0, 0)

    def finish(chunk, carry):
        at = rows(chunk)
        inside = pl.ds(pl.multiple_of(RIM + chunk * CHUNK, CHUNK), CHUNK)
        real = canvas[0, inside, 0:TILE]
        imag = canvas[1, inside, 0:TILE]
        cosine = cosv[at, :]
        sine = sinv[at, :]
        out[0, 0, at, :] = (real * cosine - imag * sine).astype(BF16)
        out[1, 0, at, :] = (real * sine + imag * cosine).astype(BF16)
        return carry

    lax.fori_loop(0, TILE // CHUNK, finish, 0)
    drain(0, "gy", rim_ways)
    drain(1, "gx", row_ways)
    drain(2, "gx", a_ways)
    drain(3, "gy", b_ways)
    drain(4, "gy", pa_ways)
    drain(5, "gx", pb_ways)
    drain(6, "gx", or_ways)
    drain(7, "gy", oc_ways)


def per_device(
    sizes, wavefield, slowness, frequencies, propagator, window_velocity_group, reach_list, coupling
):
    a1, b1, a2, b2 = (jnp.asarray(table) for table in tables())
    anywhere = pl.BlockSpec(memory_space=pl.ANY)
    scalar = pl.BlockSpec(memory_space=pltpu.SMEM)
    vmem = pltpu.VMEM
    window_half = (2, 2, 2, HALF, LENGTH)
    call = pl.pallas_call(
        functools.partial(kernel, sizes),
        out_shape=jax.ShapeDtypeStruct(wavefield.shape, BF16),
        in_specs=[anywhere, anywhere, scalar, anywhere, scalar, scalar, scalar] + [anywhere] * 4,
        out_specs=pl.BlockSpec(memory_space=pltpu.VMEM),
        scratch_shapes=[
            vmem((2, TILE, TILE), BF16),
            vmem((TILE, TILE), F32),
            vmem((3, 2, LENGTH, LENGTH), BF16),
            vmem((WIDE, WIDE), BF16),
            vmem((WIDE, WIDE), BF16),
            vmem((LENGTH, LENGTH), BF16),
            vmem((LENGTH, LENGTH), BF16),
            vmem((2, 2, RIM, TILE), BF16),
            vmem((2, 2, RIM, TILE), BF16),
            vmem((2, TILE, WIDE), F32),
            vmem((2, TILE + OVER, WIDE), BF16),
            vmem((2, 2, LENGTH, WIDE), BF16),
            vmem(window_half, BF16),
            vmem(window_half, BF16),
            vmem(window_half, BF16),
            vmem(window_half, BF16),
            vmem(window_half, BF16),
            vmem(window_half, BF16),
            vmem(window_half, BF16),
            vmem(window_half, BF16),
            vmem((2,) + window_half, F32),
            vmem((2, 2, 2, LENGTH, LENGTH), BF16),
            vmem((2, 2, LENGTH, WIDE), BF16),
            vmem((2, TILE + OVER, WIDE), F32),
            vmem((TILE, TILE), F32),
            vmem((TILE, TILE), F32),
            vmem((2, 2, RIM, WIDE), BF16),
            vmem((2, 2, RIM, WIDE), BF16),
            vmem((2, 2, RIM, TILE), BF16),
            vmem((2, 2, RIM, TILE), BF16),
            pltpu.SMEM((2 * len(NEEDED),), F32),
            pltpu.SemaphoreType.DMA((7,)),
            pltpu.SemaphoreType.DMA((16,)),
            pltpu.SemaphoreType.DMA((16,)),
        ],
        compiler_params=pltpu.CompilerParams(
            collective_id=0, has_side_effects=True, vmem_limit_bytes=60 * 1024 * 1024
        ),
    )
    return call(
        wavefield,
        slowness,
        frequencies,
        propagator,
        window_velocity_group,
        jnp.transpose(reach_list, (2, 0, 1)),
        jnp.transpose(coupling, (0, 2, 3, 1)),
        a1,
        b1,
        a2,
        b2,
    )


def solution(mesh):
    sizes = (mesh.shape["gx"], mesh.shape["gy"])
    return jax.shard_map(
        functools.partial(per_device, sizes),
        mesh=mesh,
        in_specs=(P(None, None, "gx", "gy"), P("gx", "gy"), P(), P(), P(), P(), P()),
        out_specs=P(None, None, "gx", "gy"),
        check_vma=False,
    )
```

```python
import functools

import jax
import jax.numpy as jnp
import numpy as np
from jax import lax
from jax.experimental import pallas as pl
from jax.experimental.pallas import tpu as pltpu
from jax.sharding import PartitionSpec as P

LENGTH = 256
OVER = 32
RIM = OVER // 2
STRIDE = LENGTH - OVER
TILE = 2 * STRIDE
WIDE = 2 * LENGTH
PIECE = LENGTH // 4
CHUNK = 16
BF16 = jnp.bfloat16
F32 = jnp.float32


def tables():
    points = np.arange(LENGTH) + 0.5
    cosines = np.sqrt(2.0 / LENGTH) * np.cos(np.pi / LENGTH * points[:, None] * points[None, :])
    cosines = cosines.astype(np.float32).astype(jnp.bfloat16).astype(np.float64)
    cells = np.arange(LENGTH)
    rising = np.sin(0.5 * np.pi * (cells + 0.5) / OVER)
    falling = np.cos(0.5 * np.pi * (cells - STRIDE + 0.5) / OVER)
    bell = np.where(cells < OVER, rising, np.where(cells >= STRIDE, falling, 1.0))
    tapered = cosines * bell[None, :]
    across = np.zeros((WIDE, WIDE))
    for window in range(2):
        for cell in range(LENGTH):
            at = window * STRIDE + cell - RIM
            if at < 0:
                at = TILE + at + RIM
            elif at >= TILE:
                at = RIM + at
            across[at, window * LENGTH : (window + 1) * LENGTH] = tapered[:, cell]

    def low(array):
        return np.ascontiguousarray(array).astype(np.float32).astype(jnp.bfloat16)

    order = np.arange(LENGTH).reshape(2, 2, PIECE).transpose(1, 0, 2).reshape(-1)
    return low(across), low(across.T), low(tapered), low(tapered.T[:, order])


NEEDED = []
for _tx in (0, 1):
    for _ty in (0, 1):
        NEEDED += [(_tx, _ty, _dx, _dy) for _dx in (-1, 0, 1) for _dy in (-1, 0, 1)]
for _t in (0, 1):
    NEEDED += [(_t, -1, _dx, 1) for _dx in (-1, 0, 1)]
    NEEDED += [(_t, 2, _dx, -1) for _dx in (-1, 0, 1)]
    NEEDED += [(-1, _t, 1, _dy) for _dy in (-1, 0, 1)]
    NEEDED += [(2, _t, -1, _dy) for _dy in (-1, 0, 1)]
PLACE = {key: index for index, key in enumerate(NEEDED)}


def contract(left, right, left_dim, right_dim):
    return lax.dot_general(
        left, right, (((left_dim,), (right_dim,)), ((), ())), preferred_element_type=F32
    )


def selector(rows, columns, target):
    row = lax.broadcasted_iota(jnp.int32, (rows, columns), 0)
    column = lax.broadcasted_iota(jnp.int32, (rows, columns), 1)
    return jnp.where(column == target(row), 1.0, 0.0).astype(BF16)


def sine_cosine(angle):
    turns = jnp.floor(angle * np.float32(2 / np.pi) + 0.5)
    rest = angle - turns * np.float32(1.5703125)
    rest = rest - turns * np.float32(4.837512969970703e-4)
    rest = rest - turns * np.float32(7.549789954891882e-8)
    square = rest * rest
    sine = np.float32(-1.9515295891e-4) * square + np.float32(8.3321608736e-3)
    sine = sine * square + np.float32(-1.6666654611e-1)
    sine = sine * square * rest + rest
    cosine = np.float32(2.443315711809948e-5) * square + np.float32(-1.388731625493765e-3)
    cosine = cosine * square + np.float32(4.166664568298827e-2)
    cosine = cosine * square * square + (1.0 - 0.5 * square)
    quarter = turns.astype(jnp.int32)
    swap = (quarter & 1) != 0
    first = jnp.where(swap, cosine, sine)
    second = jnp.where(swap, sine, cosine)
    first = jnp.where((quarter & 2) != 0, -first, first)
    second = jnp.where(((quarter + 1) & 2) != 0, -second, second)
    return first, second


SIDES = (-1, 1)


def lands(step):
    return 0 if step > 0 else 1


def leaves(step):
    return 1 if step > 0 else 0


def kernel(
    sizes,
    x_hbm,
    slow_hbm,
    freq,
    prop_hbm,
    group_hbm,
    reach_hbm,
    coup_hbm,
    a1_hbm,
    b1_hbm,
    a2_hbm,
    b2_hbm,
    out,
    xv,
    slow,
    big,
    a1,
    b1,
    a2,
    b2,
    hs,
    hr,
    xr,
    hc,
    fp32,
    fp,
    cf,
    swa,
    swb,
    ra,
    rb,
    pa,
    pb,
    qa,
    qb,
    acc,
    mixed,
    pg,
    second,
    canvas,
    cosv,
    sinv,
    ors,
    orr,
    ocs,
    ocr,
    occ,
    occr,
    group,
    reach,
    coup,
    weights,
    local_sem,
    send_sem,
    recv_sem,
):
    size_x, size_y = sizes
    total_x = 2 * size_x
    total_y = 2 * size_y
    gx = lax.axis_index("gx")
    gy = lax.axis_index("gy")
    has = {
        ("gx", -1): gx > 0,
        ("gx", 1): gx < size_x - 1,
        ("gy", -1): gy > 0,
        ("gy", 1): gy < size_y - 1,
    }
    here = {"gx": gx, "gy": gy}
    ways = [{"gx": step} for step in SIDES] + [{"gy": step} for step in SIDES]
    ways += [{"gx": sx, "gy": sy} for sx in SIDES for sy in SIDES]

    def exists(way, sign=1):
        found = [has[axis, sign * step] for axis, step in way.items()]
        return found[0] if len(found) == 1 else jnp.logical_and(*found)

    def device(way):
        return {axis: here[axis] + step for axis, step in way.items()}

    barrier = pltpu.get_barrier_semaphore()
    for way in ways:

        @pl.when(exists(way))
        def _(way=way):
            pl.semaphore_signal(
                barrier, inc=1, device_id=device(way), device_id_type=pl.DeviceIdType.MESH
            )

    base_x = jnp.clip(2 * gx - 1, 0, total_x - 4)
    copies = {
        "x0": [(x_hbm.at[0, 0], xv.at[0:TILE])],
        "x1": [(x_hbm.at[1, 0], xv.at[TILE:])],
        "a1": [(a1_hbm, a1)],
        "reach": [(reach_hbm, reach)],
        "coup": [(coup_hbm.at[pl.ds(base_x, 4)], coup)],
        "group": [(group_hbm, group)],
        "a2": [(a2_hbm, a2)],
    }
    for which in range(3):
        copies["real%d" % which] = [
            (prop_hbm.at[which, 0, 0], big.at[which, 0:LENGTH, 0:LENGTH]),
            (prop_hbm.at[which, 0, 0], big.at[which, LENGTH:WIDE, LENGTH:WIDE]),
            (prop_hbm.at[which, 0, 1], big.at[which, LENGTH:WIDE, 0:LENGTH]),
        ]
    copies["slow"] = [(slow_hbm, slow)]
    copies["b1"] = [(b1_hbm, b1)]
    copies["b2"] = [(b2_hbm, b2)]
    loads = {}
    number = 0
    for name, pairs in copies.items():
        loads[name] = []
        for source, target in pairs:
            loads[name].append(pltpu.make_async_copy(source, target, local_sem.at[number]))
            number += 1
    for batch in loads.values():
        for load in batch:
            load.start()

    def loaded(name):
        for load in loads[name]:
            load.wait()

    counter = [0]

    def message(way, source, target):
        counter[0] += 1
        return counter[0] - 1, way, source, target

    def copy_of(item):
        slot, way, source, target = item
        return pltpu.make_async_remote_copy(
            src_ref=source,
            dst_ref=target,
            send_sem=send_sem.at[slot],
            recv_sem=recv_sem.at[slot],
            device_id=device(way),
            device_id_type=pl.DeviceIdType.MESH,
        )

    def start(items):
        for item in items:

            @pl.when(exists(item[1]))
            def _(item=item):
                copy_of(item).start()

    def arrive(items):
        for item in items:

            @pl.when(exists(item[1], -1))
            def _(item=item):
                copy_of(item).wait_recv()

    def drain(items):
        for item in items:

            @pl.when(exists(item[1]))
            def _(item=item):
                copy_of(item).wait_send()

    def clear_missing(items):
        for item in items:

            @pl.when(jnp.logical_not(exists(item[1], -1)))
            def _(target=item[3]):
                target[...] = jnp.zeros(target.shape, target.dtype)

    row_rims = [
        message({"gx": -1}, x_hbm.at[:, 0, 0:RIM], xr.at[1]),
        message({"gx": 1}, x_hbm.at[:, 0, TILE - RIM : TILE], xr.at[0]),
    ]
    column_rims = [message({"gy": step}, hs.at[leaves(step)], hr.at[lands(step)]) for step in SIDES]
    corner_rims = [
        message(
            {"gx": sx, "gy": sy},
            hs.at[leaves(sy), :, :, 0:128] if sx < 0 else hs.at[leaves(sy), :, :, 384:512],
            hc.at[lands(sx), lands(sy)],
        )
        for sx in SIDES
        for sy in SIDES
    ]

    def sided(axis, piece, source, target):
        return [
            message({axis: step}, source.at[piece, leaves(step)], target.at[piece, lands(step)])
            for step in SIDES
        ]

    a_items = [sided("gx", piece, swa, ra) for piece in range(2)]
    b_items = [sided("gy", piece, swb, rb) for piece in range(2)]
    pa_items = [sided("gy", piece, pa, qa) for piece in range(2)]
    pb_items = [sided("gx", piece, pb, qb) for piece in range(2)]
    row_sums = [message({"gx": step}, ors.at[leaves(step)], orr.at[lands(step)]) for step in SIDES]
    column_sums = [message({"gy": step}, ocs.at[leaves(step)], ocr.at[lands(step)]) for step in SIDES]
    corner_sums = [
        message({"gx": sx, "gy": sy}, occ.at[leaves(sx)], occr.at[lands(sx), lands(sy)])
        for sx in SIDES
        for sy in SIDES
    ]

    pick = selector(OVER, TILE, lambda r: jnp.where(r < RIM, r, r + TILE - OVER))
    hs[:, :, :, 384:512] = jnp.zeros((2, 2, RIM, 128), BF16)
    for part in range(2):
        loaded("x%d" % part)
        rims = contract(pick, xv[part * TILE : (part + 1) * TILE], 1, 1).astype(BF16)
        hs[0, part, :, 0:TILE] = rims[:RIM]
        hs[1, part, :, 0:TILE] = rims[RIM:]
    for items in (row_rims, column_rims, corner_rims, row_sums, column_sums, corner_sums):
        clear_missing(items)
    pl.semaphore_wait(barrier, sum(exists(way).astype(jnp.int32) for way in ways))
    start(corner_rims)
    start(column_rims)
    start(row_rims)

    loaded("a1")
    fp32[...] = jnp.dot(xv[...], a1[:TILE], preferred_element_type=F32)

    loaded("reach")
    loaded("coup")
    for tx, ty in sorted({key[:2] for key in NEEDED}):
        at_x = 2 * gx + tx
        at_y = 2 * gy + ty
        near_x = jnp.clip(at_x, 0, total_x - 1)
        near_y = jnp.clip(at_y, 0, total_y - 1)
        row = near_x - base_x
        slots = [
            (reach[s, near_x, near_y], coup[row, s, 0, near_y], coup[row, s, 1, near_y])
            for s in range(reach.shape[0])
        ]
        for key, place in PLACE.items():
            if key[:2] != (tx, ty):
                continue
            window = (at_x + key[2]) * total_y + at_y + key[3]
            window = jnp.where(at_x + key[2] < 0, -2, window)
            real = jnp.float32(0.0)
            imag = jnp.float32(0.0)
            for entry, entry_real, entry_imag in slots:
                same = entry == window
                real = jnp.where(same, entry_real, real)
                imag = jnp.where(same, entry_imag, imag)
            weights[2 * place] = real
            weights[2 * place + 1] = imag
    for which in range(3):
        loaded("real%d" % which)
        big[which, 0:LENGTH, LENGTH:WIDE] = -big[which, LENGTH:WIDE, 0:LENGTH]
    loaded("a2")
    loaded("group")
    for piece in range(2):
        clear_missing(a_items[piece])
        clear_missing(b_items[piece])

    a1_rims = a1[TILE : TILE + OVER]
    arrive(column_rims)
    for part in range(2):
        rims = jnp.concatenate([hr[0, part, :, 0:TILE], hr[1, part, :, 0:TILE]], axis=0)
        fp[part, RIM : TILE + RIM] = (
            fp32[part * TILE : (part + 1) * TILE] + contract(rims, a1_rims, 0, 0)
        ).astype(BF16)
    arrive(row_rims)
    arrive(corner_rims)
    beyond = jnp.dot(xr[...].reshape(4 * RIM, TILE), a1[:TILE], preferred_element_type=F32)
    for side in range(2):
        corners = jnp.concatenate(
            [
                jnp.concatenate([hc[side, 0, part], hc[side, 1, part]], axis=0)
                for part in range(2)
            ],
            axis=1,
        )
        corners = contract(corners, a1_rims, 0, 0)
        skip = 48 if side == 0 else 0
        to = 0 if side == 0 else TILE + RIM
        for part in range(2):
            at = (2 * side + part) * RIM
            fp[part, to : to + RIM] = (
                beyond[at : at + RIM] + corners[part * 128 + skip : part * 128 + skip + RIM]
            ).astype(BF16)

    for wx in range(2):
        for part in range(2):
            found = jnp.dot(
                a2[...],
                fp[part, wx * STRIDE : wx * STRIDE + LENGTH],
                preferred_element_type=F32,
            ).astype(BF16)
            for wy in range(2):
                cf[wx, wy, part * LENGTH : (part + 1) * LENGTH] = found[
                    :, wy * LENGTH : (wy + 1) * LENGTH
                ]

    def group_of(wx, wy):
        return group[2 * gx + wx, 2 * gy + wy]

    for wx in range(2):
        for wy in range(2):
            swept = jnp.dot(
                big[group_of(wx, wy)], cf[wx, wy], preferred_element_type=F32
            ).astype(BF16)
            for part in range(2):
                for piece in range(2):
                    at = part * LENGTH + piece * PIECE
                    swa[piece, wx, wy, part] = swept[at : at + PIECE]
                    at = at + 2 * PIECE
                    swb[piece, wy, wx, part] = swept[at : at + PIECE]
        if wx == 0:
            start([a_items[0][0]])
    start([a_items[0][1]])
    start(b_items[0])
    start(a_items[1])
    start(b_items[1])

    def source(half, piece, x, y):
        if half == 0:
            if x in (0, 1):
                return swa.at[piece, x, y]
            return ra.at[piece, 0 if x < 0 else 1, y]
        if y in (0, 1):
            return swb.at[piece, y, x]
        return rb.at[piece, 0 if y < 0 else 1, x]

    def rows(chunk, start=0):
        return pl.ds(pl.multiple_of(start + chunk * CHUNK, CHUNK), CHUNK)

    def mix(half, piece, sums, get, put):
        def body(chunk, carry):
            at = rows(chunk)
            held = {}

            def value(x, y):
                if (x, y) not in held:
                    ref = source(half, piece, x, y)
                    held[x, y] = (ref[0, at, :].astype(F32), ref[1, at, :].astype(F32))
                return held[x, y]

            for (tx, ty), sources in sums:
                real, imag = get(tx, ty, at) if get is not None else (None, None)
                for sx, sy in sources:
                    place = PLACE[tx, ty, sx - tx, sy - ty]
                    w_real = weights[2 * place]
                    w_imag = weights[2 * place + 1]
                    v_real, v_imag = value(sx, sy)
                    add_real = w_real * v_real - w_imag * v_imag
                    add_imag = w_real * v_imag + w_imag * v_real
                    real = add_real if real is None else real + add_real
                    imag = add_imag if imag is None else imag + add_imag
                put(tx, ty, at, real, imag)
            return carry

        lax.fori_loop(0, PIECE // CHUNK, body, 0)

    def acc_get(half, piece):
        def get(tx, ty, at):
            return acc[half, piece, tx, ty, 0, at, :], acc[half, piece, tx, ty, 1, at, :]

        return get

    def acc_put(half, piece):
        def put(tx, ty, at, real, imag):
            acc[half, piece, tx, ty, 0, at, :] = real
            acc[half, piece, tx, ty, 1, at, :] = imag

        return put

    inner = [(x, y) for x in (0, 1) for y in (0, 1)]
    for piece in range(2):
        for half in range(2):
            mix(half, piece, [(target, inner) for target in inner], None, acc_put(half, piece))
        clear_missing(pa_items[piece])
        clear_missing(pb_items[piece])

    loaded("slow")

    def phase_rows(chunk, carry):
        at = rows(chunk)
        sinv[at, :], cosv[at, :] = sine_cosine(freq[0] * slow[at, :])
        return carry

    lax.fori_loop(0, TILE // CHUNK, phase_rows, 0)

    def pa_put(piece):
        def put(tx, ty, at, real, imag):
            side = 0 if ty < 0 else 1
            pa[piece, side, tx, 0, at, :] = real.astype(BF16)
            pa[piece, side, tx, 1, at, :] = imag.astype(BF16)

        return put

    def pb_put(piece):
        def put(tx, ty, at, real, imag):
            side = 0 if tx < 0 else 1
            pb[piece, side, ty, 0, at, :] = real.astype(BF16)
            pb[piece, side, ty, 1, at, :] = imag.astype(BF16)

        return put

    near = (-1, 0, 1)
    for piece in range(2):
        arrive(a_items[piece])
        mix(
            0,
            piece,
            [((t, -1), [(t + d, 0) for d in near]) for t in (0, 1)]
            + [((t, 2), [(t + d, 1) for d in near]) for t in (0, 1)],
            None,
            pa_put(piece),
        )
        start(pa_items[piece])
        arrive(b_items[piece])
        mix(
            1,
            piece,
            [((-1, t), [(0, t + d) for d in near]) for t in (0, 1)]
            + [((2, t), [(1, t + d) for d in near]) for t in (0, 1)],
            None,
            pb_put(piece),
        )
        start(pb_items[piece])
    for piece in range(2):
        mix(
            0,
            piece,
            [((0, y), [(-1, 0), (-1, 1)]) for y in (0, 1)]
            + [((1, y), [(2, 0), (2, 1)]) for y in (0, 1)],
            acc_get(0, piece),
            acc_put(0, piece),
        )
        mix(
            1,
            piece,
            [((x, 0), [(0, -1), (1, -1)]) for x in (0, 1)]
            + [((x, 1), [(0, 2), (1, 2)]) for x in (0, 1)],
            acc_get(1, piece),
            acc_put(1, piece),
        )
    loaded("b1")
    loaded("b2")

    span = 2 * PIECE
    for piece in range(2):
        arrive(pa_items[piece])
        arrive(pb_items[piece])

        def join(chunk, carry, piece=piece):
            at = rows(chunk)
            below = rows(chunk, PIECE)
            for tx, ty in inner:
                for part in range(2):
                    lanes = slice(part * LENGTH, (part + 1) * LENGTH)
                    mixed[piece, tx, ty, at, lanes] = (
                        acc[0, piece, tx, ty, part, at, :]
                        + qa[piece, ty, tx, part, at, :].astype(F32)
                    ).astype(BF16)
                    mixed[piece, tx, ty, below, lanes] = (
                        acc[1, piece, tx, ty, part, at, :]
                        + qb[piece, tx, ty, part, at, :].astype(F32)
                    ).astype(BF16)
            return carry

        lax.fori_loop(0, PIECE // CHUNK, join, 0)
        for wx in range(2):
            for wy in range(2):
                spread = contract(mixed[piece, wx, wy], big[group_of(wx, wy)], 1, 1).astype(BF16)
                for part in range(2):
                    at = (2 * wx + part) * span
                    pg[piece, at : at + span, wy * LENGTH : (wy + 1) * LENGTH] = spread[
                        :, part * LENGTH : (part + 1) * LENGTH
                    ]
        across = jnp.dot(pg[piece], b1[...], preferred_element_type=F32).astype(BF16)
        for wx in range(2):
            for part in range(2):
                at = (2 * wx + part) * span
                second[wx, part, piece * span : (piece + 1) * span] = across[at : at + span]

    for part in range(2):
        pieces = [
            jnp.dot(b2[...], second[wx, part], preferred_element_type=F32) for wx in range(2)
        ]
        canvas[part, 0:STRIDE] = pieces[0][:STRIDE]
        canvas[part, STRIDE:LENGTH] = pieces[0][STRIDE:] + pieces[1][:OVER]
        canvas[part, LENGTH : TILE + OVER] = pieces[1][OVER:]
    own = slice(RIM, TILE + RIM)
    ends = (slice(0, RIM), slice(TILE + RIM, TILE + OVER))
    for side in range(2):
        ors[side] = canvas[:, ends[side], 0:TILE].astype(BF16)
        occ[side] = canvas[:, ends[side], 384:512].astype(BF16)
    start(corner_sums)
    start(row_sums)
    pick_rim = selector(OVER, 128, lambda r: r + 64)
    for part in range(2):
        rims = contract(pick_rim, canvas[part, own, 384:512].astype(BF16), 1, 1).astype(BF16)
        ocs[0, part] = rims[:RIM]
        ocs[1, part] = rims[RIM:]
    start(column_sums)
    first = selector(RIM, 128, lambda r: r)
    last = selector(RIM, 128, lambda r: r + 48)
    edges = (slice(RIM, 2 * RIM), slice(TILE, TILE + RIM))
    lane = lax.broadcasted_iota(jnp.int32, (128, 128), 0)
    to = lax.broadcasted_iota(jnp.int32, (128, 128), 1)
    first_corner = jnp.where((to < RIM) & (lane == to + 80), 1.0, 0.0).astype(BF16)
    last_corner = jnp.where((to >= 48) & (to < 64) & (lane == to + 16), 1.0, 0.0).astype(BF16)
    arrive(row_sums)
    for side in range(2):
        canvas[:, edges[side], 0:TILE] = canvas[:, edges[side], 0:TILE] + orr[side].astype(F32)
    arrive(corner_sums)
    for side in range(2):
        for part in range(2):
            canvas[part, edges[side], 0:128] = canvas[part, edges[side], 0:128] + contract(
                occr[side, 0, part], first_corner, 1, 0
            )
            canvas[part, edges[side], 384:512] = canvas[part, edges[side], 384:512] + contract(
                occr[side, 1, part], last_corner, 1, 0
            )
    arrive(column_sums)
    for part in range(2):
        canvas[part, own, 0:128] = canvas[part, own, 0:128] + contract(ocr[0, part], first, 0, 0)
        canvas[part, own, 384:512] = canvas[part, own, 384:512] + contract(ocr[1, part], last, 0, 0)

    def finish(chunk, carry):
        at = rows(chunk)
        inside = rows(chunk, RIM)
        real = canvas[0, inside, 0:TILE]
        imag = canvas[1, inside, 0:TILE]
        cosine = cosv[at, :]
        sine = sinv[at, :]
        out[0, 0, at, :] = (real * cosine - imag * sine).astype(BF16)
        out[1, 0, at, :] = (real * sine + imag * cosine).astype(BF16)
        return carry

    lax.fori_loop(0, TILE // CHUNK, finish, 0)
    for items in [row_rims, column_rims, corner_rims, row_sums, column_sums, corner_sums]:
        drain(items)
    for piece in range(2):
        for items in (a_items, b_items, pa_items, pb_items):
            drain(items[piece])


def per_device(
    sizes, wavefield, slowness, frequencies, propagator, window_velocity_group, reach_list, coupling
):
    a1, b1, a2, b2 = (jnp.asarray(table) for table in tables())
    anywhere = pl.BlockSpec(memory_space=pl.ANY)
    vmem = pltpu.VMEM
    pieces = (2, 2, 2, 2, PIECE, LENGTH)
    groups, slots = propagator.shape[0], reach_list.shape[2]
    call = pl.pallas_call(
        functools.partial(kernel, sizes),
        out_shape=jax.ShapeDtypeStruct(wavefield.shape, BF16),
        in_specs=[anywhere, anywhere, pl.BlockSpec(memory_space=pltpu.SMEM)] + [anywhere] * 8,
        out_specs=pl.BlockSpec(memory_space=pltpu.VMEM),
        scratch_shapes=[
            vmem((2 * TILE, TILE), BF16),
            vmem((TILE, TILE), F32),
            vmem((groups, WIDE, WIDE), BF16),
            vmem((WIDE, WIDE), BF16),
            vmem((WIDE, WIDE), BF16),
            vmem((LENGTH, LENGTH), BF16),
            vmem((LENGTH, LENGTH), BF16),
            vmem((2, 2, RIM, WIDE), BF16),
            vmem((2, 2, RIM, WIDE), BF16),
            vmem((2, 2, RIM, TILE), BF16),
            vmem((2, 2, 2, RIM, 128), BF16),
            vmem((2 * TILE, WIDE), F32),
            vmem((2, TILE + OVER, WIDE), BF16),
            vmem((2, 2, WIDE, LENGTH), BF16),
        ]
        + [vmem(pieces, BF16)] * 8
        + [
            vmem((2, 2, 2, 2, 2, PIECE, LENGTH), F32),
            vmem((2, 2, 2, 2 * PIECE, WIDE), BF16),
            vmem((2, 8 * PIECE, WIDE), BF16),
            vmem((2, 2, LENGTH, WIDE), BF16),
            vmem((2, TILE + OVER, WIDE), F32),
            vmem((TILE, TILE), F32),
            vmem((TILE, TILE), F32),
            vmem((2, 2, RIM, TILE), BF16),
            vmem((2, 2, RIM, TILE), BF16),
            vmem((2, 2, RIM, TILE), BF16),
            vmem((2, 2, RIM, TILE), BF16),
            vmem((2, 2, RIM, 128), BF16),
            vmem((2, 2, 2, RIM, 128), BF16),
            pltpu.SMEM(window_velocity_group.shape, jnp.int32),
            pltpu.SMEM((slots, *reach_list.shape[:2]), jnp.int32),
            pltpu.SMEM((4, slots, 2, coupling.shape[1]), F32),
            pltpu.SMEM((2 * len(NEEDED),), F32),
            pltpu.SemaphoreType.DMA((19,)),
            pltpu.SemaphoreType.DMA((32,)),
            pltpu.SemaphoreType.DMA((32,)),
        ],
        compiler_params=pltpu.CompilerParams(
            collective_id=0, has_side_effects=True, vmem_limit_bytes=60 * 1024 * 1024
        ),
    )
    return call(
        wavefield,
        slowness,
        frequencies,
        propagator,
        window_velocity_group,
        jnp.transpose(reach_list, (2, 0, 1)),
        jnp.transpose(coupling, (0, 2, 3, 1)),
        a1,
        b1,
        a2,
        b2,
    )


def solution(mesh):
    sizes = (mesh.shape["gx"], mesh.shape["gy"])
    return jax.shard_map(
        functools.partial(per_device, sizes),
        mesh=mesh,
        in_specs=(P(None, None, "gx", "gy"), P("gx", "gy"), P(), P(), P(), P(), P()),
        out_specs=P(None, None, "gx", "gy"),
        check_vma=False,
    )
```

```python
import functools

import jax
import jax.numpy as jnp
import numpy as np
from jax import lax
from jax.experimental import pallas as pl
from jax.experimental.pallas import tpu as pltpu
from jax.sharding import PartitionSpec as P

LENGTH = 256
OVER = 32
RIM = OVER // 2
STRIDE = LENGTH - OVER
TILE = 2 * STRIDE
WIDE = 2 * LENGTH
PIECE = LENGTH // 4
CHUNK = 16
BF16 = jnp.bfloat16
F32 = jnp.float32


def tables():
    points = np.arange(LENGTH) + 0.5
    cosines = np.sqrt(2.0 / LENGTH) * np.cos(np.pi / LENGTH * points[:, None] * points[None, :])
    cosines = cosines.astype(np.float32).astype(jnp.bfloat16).astype(np.float64)
    cells = np.arange(LENGTH)
    rising = np.sin(0.5 * np.pi * (cells + 0.5) / OVER)
    falling = np.cos(0.5 * np.pi * (cells - STRIDE + 0.5) / OVER)
    bell = np.where(cells < OVER, rising, np.where(cells >= STRIDE, falling, 1.0))
    tapered = cosines * bell[None, :]
    across = np.zeros((WIDE, WIDE))
    for window in range(2):
        for cell in range(LENGTH):
            at = window * STRIDE + cell - RIM
            if at < 0:
                at = TILE + at + RIM
            elif at >= TILE:
                at = RIM + at
            across[at, window * LENGTH : (window + 1) * LENGTH] = tapered[:, cell]

    def low(array):
        return np.ascontiguousarray(array).astype(np.float32).astype(jnp.bfloat16)

    order = np.arange(LENGTH).reshape(2, 2, PIECE).transpose(1, 0, 2).reshape(-1)
    return low(across), low(across.T), low(tapered), low(tapered.T[:, order])


NEEDED = []
for _tx in (0, 1):
    for _ty in (0, 1):
        NEEDED += [(_tx, _ty, _dx, _dy) for _dx in (-1, 0, 1) for _dy in (-1, 0, 1)]
for _t in (0, 1):
    NEEDED += [(_t, -1, _dx, 1) for _dx in (-1, 0, 1)]
    NEEDED += [(_t, 2, _dx, -1) for _dx in (-1, 0, 1)]
    NEEDED += [(-1, _t, 1, _dy) for _dy in (-1, 0, 1)]
    NEEDED += [(2, _t, -1, _dy) for _dy in (-1, 0, 1)]
PLACE = {key: index for index, key in enumerate(NEEDED)}


def contract(left, right, left_dim, right_dim):
    return lax.dot_general(
        left, right, (((left_dim,), (right_dim,)), ((), ())), preferred_element_type=F32
    )


def selector(rows, columns, target):
    row = lax.broadcasted_iota(jnp.int32, (rows, columns), 0)
    column = lax.broadcasted_iota(jnp.int32, (rows, columns), 1)
    return jnp.where(column == target(row), 1.0, 0.0).astype(BF16)


def sine_cosine(angle):
    turns = jnp.floor(angle * np.float32(2 / np.pi) + 0.5)
    rest = angle - turns * np.float32(1.5703125)
    rest = rest - turns * np.float32(4.837512969970703e-4)
    rest = rest - turns * np.float32(7.549789954891882e-8)
    square = rest * rest
    sine = np.float32(-1.9515295891e-4) * square + np.float32(8.3321608736e-3)
    sine = sine * square + np.float32(-1.6666654611e-1)
    sine = sine * square * rest + rest
    cosine = np.float32(2.443315711809948e-5) * square + np.float32(-1.388731625493765e-3)
    cosine = cosine * square + np.float32(4.166664568298827e-2)
    cosine = cosine * square * square + (1.0 - 0.5 * square)
    quarter = turns.astype(jnp.int32)
    swap = (quarter & 1) != 0
    first = jnp.where(swap, cosine, sine)
    second = jnp.where(swap, sine, cosine)
    first = jnp.where((quarter & 2) != 0, -first, first)
    second = jnp.where(((quarter + 1) & 2) != 0, -second, second)
    return first, second


SIDES = (-1, 1)


def lands(step):
    return 0 if step > 0 else 1


def leaves(step):
    return 1 if step > 0 else 0


def kernel(
    sizes,
    x_hbm,
    slow_hbm,
    freq,
    prop_hbm,
    group_hbm,
    reach_hbm,
    coup_hbm,
    a1_hbm,
    b1_hbm,
    a2_hbm,
    b2_hbm,
    out,
    xv,
    slow,
    big,
    a1,
    b1,
    a2,
    b2,
    hs,
    hr,
    xr,
    hc,
    fp32,
    fp,
    cf,
    swa,
    swb,
    ra,
    rb,
    pa,
    pb,
    qa,
    qb,
    acc,
    mixed,
    pg,
    second,
    canvas,
    cosv,
    sinv,
    ors,
    orr,
    ocs,
    ocr,
    occ,
    occr,
    group,
    reach,
    coup,
    weights,
    held,
    local_sem,
    send_sem,
    recv_sem,
    pass_send,
    pass_recv,
):
    size_x, size_y = sizes
    total_x = 2 * size_x
    total_y = 2 * size_y
    gx = lax.axis_index("gx")
    gy = lax.axis_index("gy")
    has = {
        ("gx", -1): gx > 0,
        ("gx", 1): gx < size_x - 1,
        ("gy", -1): gy > 0,
        ("gy", 1): gy < size_y - 1,
    }
    here = {"gx": gx, "gy": gy}
    ways = [{"gx": step} for step in SIDES] + [{"gy": step} for step in SIDES]
    ways += [{"gx": sx, "gy": sy} for sx in SIDES for sy in SIDES]

    def exists(way, sign=1):
        found = [has[axis, sign * step] for axis, step in way.items()]
        return found[0] if len(found) == 1 else jnp.logical_and(*found)

    def device(way):
        return {axis: here[axis] + step for axis, step in way.items()}

    half_x = size_x // 2
    relays = size_x % 2 == 0 and size_y % 4 == 0
    odd = lax.rem(gy, 2) == 1
    other = gy + 2 - 4 * lax.rem(lax.div(gy, 2), 2)
    leaving = {1: gx == half_x - 1, -1: gx == half_x}
    relayed = {step: jnp.logical_and(odd, leaving[step]) for step in SIDES}

    barrier = pltpu.get_barrier_semaphore()
    if relays:
        for step in SIDES:

            @pl.when(relayed[step])
            def _(step=step):
                for target in ({"gx": gx + step, "gy": other}, {"gy": other}):
                    pl.semaphore_signal(
                        barrier, inc=1, device_id=target, device_id_type=pl.DeviceIdType.MESH
                    )

    for way in ways:

        @pl.when(exists(way))
        def _(way=way):
            pl.semaphore_signal(
                barrier, inc=1, device_id=device(way), device_id_type=pl.DeviceIdType.MESH
            )

    base_x = jnp.clip(2 * gx - 1, 0, total_x - 4)
    copies = {
        "x0": [(x_hbm.at[0, 0], xv.at[0:TILE])],
        "x1": [(x_hbm.at[1, 0], xv.at[TILE:])],
        "a1": [(a1_hbm, a1)],
        "reach": [(reach_hbm, reach)],
        "coup": [(coup_hbm.at[pl.ds(base_x, 4)], coup)],
        "group": [(group_hbm, group)],
        "a2": [(a2_hbm, a2)],
    }
    for which in range(3):
        copies["real%d" % which] = [
            (prop_hbm.at[which, 0, 0], big.at[which, 0:LENGTH, 0:LENGTH]),
            (prop_hbm.at[which, 0, 0], big.at[which, LENGTH:WIDE, LENGTH:WIDE]),
            (prop_hbm.at[which, 0, 1], big.at[which, LENGTH:WIDE, 0:LENGTH]),
        ]
    copies["slow"] = [(slow_hbm, slow)]
    copies["b1"] = [(b1_hbm, b1)]
    copies["b2"] = [(b2_hbm, b2)]
    loads = {}
    number = 0
    for name, pairs in copies.items():
        loads[name] = []
        for source, target in pairs:
            loads[name].append(pltpu.make_async_copy(source, target, local_sem.at[number]))
            number += 1
    for batch in loads.values():
        for load in batch:
            load.start()

    def loaded(name):
        for load in loads[name]:
            load.wait()

    counter = [0]

    def message(way, source, target):
        counter[0] += 1
        return counter[0] - 1, way, source, target

    def copy_of(item):
        slot, way, source, target = item
        return pltpu.make_async_remote_copy(
            src_ref=source,
            dst_ref=target,
            send_sem=send_sem.at[slot],
            recv_sem=recv_sem.at[slot],
            device_id=device(way),
            device_id_type=pl.DeviceIdType.MESH,
        )

    def start(items):
        for item in items:

            @pl.when(exists(item[1]))
            def _(item=item):
                copy_of(item).start()

    def detour(item, place):
        slot, way, source, _ = item
        return pltpu.make_async_remote_copy(
            src_ref=source,
            dst_ref=held.at[place],
            send_sem=send_sem.at[slot],
            recv_sem=pass_recv.at[place],
            device_id={"gx": gx + way["gx"], "gy": other},
            device_id_type=pl.DeviceIdType.MESH,
        )

    def onward(item, place):
        slot, _, _, target = item
        return pltpu.make_async_remote_copy(
            src_ref=held.at[place],
            dst_ref=target,
            send_sem=pass_send.at[place],
            recv_sem=recv_sem.at[slot],
            device_id={"gy": other},
            device_id_type=pl.DeviceIdType.MESH,
        )

    def start_long(items, place):
        if not relays:
            start(items)
            return
        for item in items:
            step = item[1]["gx"]

            @pl.when(jnp.logical_and(exists(item[1]), jnp.logical_not(relayed[step])))
            def _(item=item):
                copy_of(item).start()

            @pl.when(relayed[step])
            def _(item=item):
                detour(item, place).start()

    def pass_on(items, place):
        if not relays:
            return
        for item in items:

            @pl.when(relayed[-item[1]["gx"]])
            def _(item=item):
                detour(item, place).wait_recv()
                onward(item, place).start()

    def passed(items, place):
        if not relays:
            return
        for item in items:

            @pl.when(relayed[-item[1]["gx"]])
            def _(item=item):
                onward(item, place).wait_send()

    def arrive(items):
        for item in items:

            @pl.when(exists(item[1], -1))
            def _(item=item):
                copy_of(item).wait_recv()

    def drain(items):
        for item in items:

            @pl.when(exists(item[1]))
            def _(item=item):
                copy_of(item).wait_send()

    def clear_missing(items):
        for item in items:

            @pl.when(jnp.logical_not(exists(item[1], -1)))
            def _(target=item[3]):
                target[...] = jnp.zeros(target.shape, target.dtype)

    row_rims = [
        message({"gx": -1}, x_hbm.at[:, 0, 0:RIM], xr.at[1]),
        message({"gx": 1}, x_hbm.at[:, 0, TILE - RIM : TILE], xr.at[0]),
    ]
    column_rims = [message({"gy": step}, hs.at[leaves(step)], hr.at[lands(step)]) for step in SIDES]
    corner_rims = [
        message(
            {"gx": sx, "gy": sy},
            hs.at[leaves(sy), :, :, 0:128] if sx < 0 else hs.at[leaves(sy), :, :, 384:512],
            hc.at[lands(sx), lands(sy)],
        )
        for sx in SIDES
        for sy in SIDES
    ]

    def sided(axis, piece, source, target):
        return [
            message({axis: step}, source.at[piece, leaves(step)], target.at[piece, lands(step)])
            for step in SIDES
        ]

    a_items = [sided("gx", piece, swa, ra) for piece in range(2)]
    b_items = [sided("gy", piece, swb, rb) for piece in range(2)]
    pa_items = [sided("gy", piece, pa, qa) for piece in range(2)]
    pb_items = [sided("gx", piece, pb, qb) for piece in range(2)]
    row_sums = [message({"gx": step}, ors.at[leaves(step)], orr.at[lands(step)]) for step in SIDES]
    column_sums = [message({"gy": step}, ocs.at[leaves(step)], ocr.at[lands(step)]) for step in SIDES]
    corner_sums = [
        message({"gx": sx, "gy": sy}, occ.at[leaves(sx)], occr.at[lands(sx), lands(sy)])
        for sx in SIDES
        for sy in SIDES
    ]

    pick = selector(OVER, TILE, lambda r: jnp.where(r < RIM, r, r + TILE - OVER))
    hs[:, :, :, 384:512] = jnp.zeros((2, 2, RIM, 128), BF16)
    for part in range(2):
        loaded("x%d" % part)
        rims = contract(pick, xv[part * TILE : (part + 1) * TILE], 1, 1).astype(BF16)
        hs[0, part, :, 0:TILE] = rims[:RIM]
        hs[1, part, :, 0:TILE] = rims[RIM:]
    for items in (row_rims, column_rims, corner_rims, row_sums, column_sums, corner_sums):
        clear_missing(items)
    expected = sum(exists(way).astype(jnp.int32) for way in ways)
    if relays:
        expected = expected + sum(2 * relayed[step].astype(jnp.int32) for step in SIDES)
    pl.semaphore_wait(barrier, expected)
    start(corner_rims)
    start(column_rims)
    start(row_rims)

    loaded("a1")
    fp32[...] = jnp.dot(xv[...], a1[:TILE], preferred_element_type=F32)

    loaded("reach")
    loaded("coup")
    for tx, ty in sorted({key[:2] for key in NEEDED}):
        at_x = 2 * gx + tx
        at_y = 2 * gy + ty
        near_x = jnp.clip(at_x, 0, total_x - 1)
        near_y = jnp.clip(at_y, 0, total_y - 1)
        row = near_x - base_x
        slots = [
            (reach[s, near_x, near_y], coup[row, s, 0, near_y], coup[row, s, 1, near_y])
            for s in range(reach.shape[0])
        ]
        for key, place in PLACE.items():
            if key[:2] != (tx, ty):
                continue
            window = (at_x + key[2]) * total_y + at_y + key[3]
            window = jnp.where(at_x + key[2] < 0, -2, window)
            real = jnp.float32(0.0)
            imag = jnp.float32(0.0)
            for entry, entry_real, entry_imag in slots:
                same = entry == window
                real = jnp.where(same, entry_real, real)
                imag = jnp.where(same, entry_imag, imag)
            weights[2 * place] = real
            weights[2 * place + 1] = imag
    for which in range(3):
        loaded("real%d" % which)
        big[which, 0:LENGTH, LENGTH:WIDE] = -big[which, LENGTH:WIDE, 0:LENGTH]
    loaded("a2")
    loaded("group")
    for piece in range(2):
        clear_missing(a_items[piece])
        clear_missing(b_items[piece])

    a1_rims = a1[TILE : TILE + OVER]
    arrive(column_rims)
    for part in range(2):
        rims = jnp.concatenate([hr[0, part, :, 0:TILE], hr[1, part, :, 0:TILE]], axis=0)
        fp[part, RIM : TILE + RIM] = (
            fp32[part * TILE : (part + 1) * TILE] + contract(rims, a1_rims, 0, 0)
        ).astype(BF16)
    arrive(row_rims)
    arrive(corner_rims)
    beyond = jnp.dot(xr[...].reshape(4 * RIM, TILE), a1[:TILE], preferred_element_type=F32)
    for side in range(2):
        corners = jnp.concatenate(
            [
                jnp.concatenate([hc[side, 0, part], hc[side, 1, part]], axis=0)
                for part in range(2)
            ],
            axis=1,
        )
        corners = contract(corners, a1_rims, 0, 0)
        skip = 48 if side == 0 else 0
        to = 0 if side == 0 else TILE + RIM
        for part in range(2):
            at = (2 * side + part) * RIM
            fp[part, to : to + RIM] = (
                beyond[at : at + RIM] + corners[part * 128 + skip : part * 128 + skip + RIM]
            ).astype(BF16)

    for wx in range(2):
        for part in range(2):
            found = jnp.dot(
                a2[...],
                fp[part, wx * STRIDE : wx * STRIDE + LENGTH],
                preferred_element_type=F32,
            ).astype(BF16)
            for wy in range(2):
                cf[wx, wy, part * LENGTH : (part + 1) * LENGTH] = found[
                    :, wy * LENGTH : (wy + 1) * LENGTH
                ]

    def group_of(wx, wy):
        return group[2 * gx + wx, 2 * gy + wy]

    for wx in range(2):
        for wy in range(2):
            swept = jnp.dot(
                big[group_of(wx, wy)], cf[wx, wy], preferred_element_type=F32
            ).astype(BF16)
            for part in range(2):
                for piece in range(2):
                    at = part * LENGTH + piece * PIECE
                    swa[piece, wx, wy, part] = swept[at : at + PIECE]
                    at = at + 2 * PIECE
                    swb[piece, wy, wx, part] = swept[at : at + PIECE]
        if wx == 0:
            start_long([a_items[0][0]], 0)
    start_long([a_items[0][1]], 0)
    start(b_items[0])
    start_long(a_items[1], 1)
    start(b_items[1])

    def source(half, piece, x, y):
        if half == 0:
            if x in (0, 1):
                return swa.at[piece, x, y]
            return ra.at[piece, 0 if x < 0 else 1, y]
        if y in (0, 1):
            return swb.at[piece, y, x]
        return rb.at[piece, 0 if y < 0 else 1, x]

    def rows(chunk, start=0):
        return pl.ds(pl.multiple_of(start + chunk * CHUNK, CHUNK), CHUNK)

    def mix(half, piece, sums, get, put):
        def body(chunk, carry):
            at = rows(chunk)
            held = {}

            def value(x, y):
                if (x, y) not in held:
                    ref = source(half, piece, x, y)
                    held[x, y] = (ref[0, at, :].astype(F32), ref[1, at, :].astype(F32))
                return held[x, y]

            for (tx, ty), sources in sums:
                real, imag = get(tx, ty, at) if get is not None else (None, None)
                for sx, sy in sources:
                    place = PLACE[tx, ty, sx - tx, sy - ty]
                    w_real = weights[2 * place]
                    w_imag = weights[2 * place + 1]
                    v_real, v_imag = value(sx, sy)
                    add_real = w_real * v_real - w_imag * v_imag
                    add_imag = w_real * v_imag + w_imag * v_real
                    real = add_real if real is None else real + add_real
                    imag = add_imag if imag is None else imag + add_imag
                put(tx, ty, at, real, imag)
            return carry

        lax.fori_loop(0, PIECE // CHUNK, body, 0)

    def acc_get(half, piece):
        def get(tx, ty, at):
            return acc[half, piece, tx, ty, 0, at, :], acc[half, piece, tx, ty, 1, at, :]

        return get

    def acc_put(half, piece):
        def put(tx, ty, at, real, imag):
            acc[half, piece, tx, ty, 0, at, :] = real
            acc[half, piece, tx, ty, 1, at, :] = imag

        return put

    inner = [(x, y) for x in (0, 1) for y in (0, 1)]
    for piece in range(2):
        for half in range(2):
            mix(half, piece, [(target, inner) for target in inner], None, acc_put(half, piece))
        clear_missing(pa_items[piece])
        clear_missing(pb_items[piece])

    loaded("slow")

    def phase_rows(chunk, carry):
        at = rows(chunk)
        sinv[at, :], cosv[at, :] = sine_cosine(freq[0] * slow[at, :])
        return carry

    lax.fori_loop(0, TILE // CHUNK, phase_rows, 0)
    pass_on(a_items[0], 0)
    pass_on(a_items[1], 1)

    def pa_put(piece):
        def put(tx, ty, at, real, imag):
            side = 0 if ty < 0 else 1
            pa[piece, side, tx, 0, at, :] = real.astype(BF16)
            pa[piece, side, tx, 1, at, :] = imag.astype(BF16)

        return put

    def pb_put(piece):
        def put(tx, ty, at, real, imag):
            side = 0 if tx < 0 else 1
            pb[piece, side, ty, 0, at, :] = real.astype(BF16)
            pb[piece, side, ty, 1, at, :] = imag.astype(BF16)

        return put

    near = (-1, 0, 1)
    for piece in range(2):
        arrive(a_items[piece])
        mix(
            0,
            piece,
            [((t, -1), [(t + d, 0) for d in near]) for t in (0, 1)]
            + [((t, 2), [(t + d, 1) for d in near]) for t in (0, 1)],
            None,
            pa_put(piece),
        )
        start(pa_items[piece])
        arrive(b_items[piece])
        mix(
            1,
            piece,
            [((-1, t), [(0, t + d) for d in near]) for t in (0, 1)]
            + [((2, t), [(1, t + d) for d in near]) for t in (0, 1)],
            None,
            pb_put(piece),
        )
        start_long(pb_items[piece], 2 + piece)
    pass_on(pb_items[0], 2)
    for piece in range(2):
        mix(
            0,
            piece,
            [((0, y), [(-1, 0), (-1, 1)]) for y in (0, 1)]
            + [((1, y), [(2, 0), (2, 1)]) for y in (0, 1)],
            acc_get(0, piece),
            acc_put(0, piece),
        )
        mix(
            1,
            piece,
            [((x, 0), [(0, -1), (1, -1)]) for x in (0, 1)]
            + [((x, 1), [(0, 2), (1, 2)]) for x in (0, 1)],
            acc_get(1, piece),
            acc_put(1, piece),
        )
    pass_on(pb_items[1], 3)
    loaded("b1")
    loaded("b2")

    span = 2 * PIECE
    for piece in range(2):
        arrive(pa_items[piece])
        arrive(pb_items[piece])

        def join(chunk, carry, piece=piece):
            at = rows(chunk)
            below = rows(chunk, PIECE)
            for tx, ty in inner:
                for part in range(2):
                    lanes = slice(part * LENGTH, (part + 1) * LENGTH)
                    mixed[piece, tx, ty, at, lanes] = (
                        acc[0, piece, tx, ty, part, at, :]
                        + qa[piece, ty, tx, part, at, :].astype(F32)
                    ).astype(BF16)
                    mixed[piece, tx, ty, below, lanes] = (
                        acc[1, piece, tx, ty, part, at, :]
                        + qb[piece, tx, ty, part, at, :].astype(F32)
                    ).astype(BF16)
            return carry

        lax.fori_loop(0, PIECE // CHUNK, join, 0)
        for wx in range(2):
            for wy in range(2):
                spread = contract(mixed[piece, wx, wy], big[group_of(wx, wy)], 1, 1).astype(BF16)
                for part in range(2):
                    at = (2 * wx + part) * span
                    pg[piece, at : at + span, wy * LENGTH : (wy + 1) * LENGTH] = spread[
                        :, part * LENGTH : (part + 1) * LENGTH
                    ]
        across = jnp.dot(pg[piece], b1[...], preferred_element_type=F32).astype(BF16)
        for wx in range(2):
            for part in range(2):
                at = (2 * wx + part) * span
                second[wx, part, piece * span : (piece + 1) * span] = across[at : at + span]

    for part in range(2):
        pieces = [
            jnp.dot(b2[...], second[wx, part], preferred_element_type=F32) for wx in range(2)
        ]
        canvas[part, 0:STRIDE] = pieces[0][:STRIDE]
        canvas[part, STRIDE:LENGTH] = pieces[0][STRIDE:] + pieces[1][:OVER]
        canvas[part, LENGTH : TILE + OVER] = pieces[1][OVER:]
    own = slice(RIM, TILE + RIM)
    ends = (slice(0, RIM), slice(TILE + RIM, TILE + OVER))
    for side in range(2):
        ors[side] = canvas[:, ends[side], 0:TILE].astype(BF16)
        occ[side] = canvas[:, ends[side], 384:512].astype(BF16)
    start(corner_sums)
    start(row_sums)
    pick_rim = selector(OVER, 128, lambda r: r + 64)
    for part in range(2):
        rims = contract(pick_rim, canvas[part, own, 384:512].astype(BF16), 1, 1).astype(BF16)
        ocs[0, part] = rims[:RIM]
        ocs[1, part] = rims[RIM:]
    start(column_sums)
    first = selector(RIM, 128, lambda r: r)
    last = selector(RIM, 128, lambda r: r + 48)
    edges = (slice(RIM, 2 * RIM), slice(TILE, TILE + RIM))
    lane = lax.broadcasted_iota(jnp.int32, (128, 128), 0)
    to = lax.broadcasted_iota(jnp.int32, (128, 128), 1)
    first_corner = jnp.where((to < RIM) & (lane == to + 80), 1.0, 0.0).astype(BF16)
    last_corner = jnp.where((to >= 48) & (to < 64) & (lane == to + 16), 1.0, 0.0).astype(BF16)
    arrive(row_sums)
    for side in range(2):
        canvas[:, edges[side], 0:TILE] = canvas[:, edges[side], 0:TILE] + orr[side].astype(F32)
    arrive(corner_sums)
    for side in range(2):
        for part in range(2):
            canvas[part, edges[side], 0:128] = canvas[part, edges[side], 0:128] + contract(
                occr[side, 0, part], first_corner, 1, 0
            )
            canvas[part, edges[side], 384:512] = canvas[part, edges[side], 384:512] + contract(
                occr[side, 1, part], last_corner, 1, 0
            )
    arrive(column_sums)
    for part in range(2):
        canvas[part, own, 0:128] = canvas[part, own, 0:128] + contract(ocr[0, part], first, 0, 0)
        canvas[part, own, 384:512] = canvas[part, own, 384:512] + contract(ocr[1, part], last, 0, 0)

    def finish(chunk, carry):
        at = rows(chunk)
        inside = rows(chunk, RIM)
        real = canvas[0, inside, 0:TILE]
        imag = canvas[1, inside, 0:TILE]
        cosine = cosv[at, :]
        sine = sinv[at, :]
        out[0, 0, at, :] = (real * cosine - imag * sine).astype(BF16)
        out[1, 0, at, :] = (real * sine + imag * cosine).astype(BF16)
        return carry

    lax.fori_loop(0, TILE // CHUNK, finish, 0)
    for items in [row_rims, column_rims, corner_rims, row_sums, column_sums, corner_sums]:
        drain(items)
    for piece in range(2):
        for items in (a_items, b_items, pa_items, pb_items):
            drain(items[piece])
        passed(a_items[piece], piece)
        passed(pb_items[piece], 2 + piece)


def per_device(
    sizes, wavefield, slowness, frequencies, propagator, window_velocity_group, reach_list, coupling
):
    a1, b1, a2, b2 = (jnp.asarray(table) for table in tables())
    anywhere = pl.BlockSpec(memory_space=pl.ANY)
    vmem = pltpu.VMEM
    pieces = (2, 2, 2, 2, PIECE, LENGTH)
    groups, slots = propagator.shape[0], reach_list.shape[2]
    call = pl.pallas_call(
        functools.partial(kernel, sizes),
        out_shape=jax.ShapeDtypeStruct(wavefield.shape, BF16),
        in_specs=[anywhere, anywhere, pl.BlockSpec(memory_space=pltpu.SMEM)] + [anywhere] * 8,
        out_specs=pl.BlockSpec(memory_space=pltpu.VMEM),
        scratch_shapes=[
            vmem((2 * TILE, TILE), BF16),
            vmem((TILE, TILE), F32),
            vmem((groups, WIDE, WIDE), BF16),
            vmem((WIDE, WIDE), BF16),
            vmem((WIDE, WIDE), BF16),
            vmem((LENGTH, LENGTH), BF16),
            vmem((LENGTH, LENGTH), BF16),
            vmem((2, 2, RIM, WIDE), BF16),
            vmem((2, 2, RIM, WIDE), BF16),
            vmem((2, 2, RIM, TILE), BF16),
            vmem((2, 2, 2, RIM, 128), BF16),
            vmem((2 * TILE, WIDE), F32),
            vmem((2, TILE + OVER, WIDE), BF16),
            vmem((2, 2, WIDE, LENGTH), BF16),
        ]
        + [vmem(pieces, BF16)] * 8
        + [
            vmem((2, 2, 2, 2, 2, PIECE, LENGTH), F32),
            vmem((2, 2, 2, 2 * PIECE, WIDE), BF16),
            vmem((2, 8 * PIECE, WIDE), BF16),
            vmem((2, 2, LENGTH, WIDE), BF16),
            vmem((2, TILE + OVER, WIDE), F32),
            vmem((TILE, TILE), F32),
            vmem((TILE, TILE), F32),
            vmem((2, 2, RIM, TILE), BF16),
            vmem((2, 2, RIM, TILE), BF16),
            vmem((2, 2, RIM, TILE), BF16),
            vmem((2, 2, RIM, TILE), BF16),
            vmem((2, 2, RIM, 128), BF16),
            vmem((2, 2, 2, RIM, 128), BF16),
            pltpu.SMEM(window_velocity_group.shape, jnp.int32),
            pltpu.SMEM((slots, *reach_list.shape[:2]), jnp.int32),
            pltpu.SMEM((4, slots, 2, coupling.shape[1]), F32),
            pltpu.SMEM((2 * len(NEEDED),), F32),
            vmem((4, 2, 2, PIECE, LENGTH), BF16),
            pltpu.SemaphoreType.DMA((19,)),
            pltpu.SemaphoreType.DMA((32,)),
            pltpu.SemaphoreType.DMA((32,)),
            pltpu.SemaphoreType.DMA((4,)),
            pltpu.SemaphoreType.DMA((4,)),
        ],
        compiler_params=pltpu.CompilerParams(
            collective_id=0, has_side_effects=True, vmem_limit_bytes=60 * 1024 * 1024
        ),
    )
    return call(
        wavefield,
        slowness,
        frequencies,
        propagator,
        window_velocity_group,
        jnp.transpose(reach_list, (2, 0, 1)),
        jnp.transpose(coupling, (0, 2, 3, 1)),
        a1,
        b1,
        a2,
        b2,
    )


def solution(mesh):
    sizes = (mesh.shape["gx"], mesh.shape["gy"])
    return jax.shard_map(
        functools.partial(per_device, sizes),
        mesh=mesh,
        in_specs=(P(None, None, "gx", "gy"), P("gx", "gy"), P(), P(), P(), P(), P()),
        out_specs=P(None, None, "gx", "gy"),
        check_vma=False,
    )
```

```python
import functools

import jax
import jax.numpy as jnp
import numpy as np
from jax import lax
from jax.experimental import pallas as pl
from jax.experimental.pallas import tpu as pltpu
from jax.sharding import PartitionSpec as P

LENGTH = 256
OVER = 32
RIM = OVER // 2
STRIDE = LENGTH - OVER
TILE = 2 * STRIDE
WIDE = 2 * LENGTH
PIECE = LENGTH // 4
CHUNK = 16
BF16 = jnp.bfloat16
F32 = jnp.float32


def tables():
    points = np.arange(LENGTH) + 0.5
    cosines = np.sqrt(2.0 / LENGTH) * np.cos(np.pi / LENGTH * points[:, None] * points[None, :])
    cosines = cosines.astype(np.float32).astype(jnp.bfloat16).astype(np.float64)
    cells = np.arange(LENGTH)
    rising = np.sin(0.5 * np.pi * (cells + 0.5) / OVER)
    falling = np.cos(0.5 * np.pi * (cells - STRIDE + 0.5) / OVER)
    bell = np.where(cells < OVER, rising, np.where(cells >= STRIDE, falling, 1.0))
    tapered = cosines * bell[None, :]
    across = np.zeros((WIDE, WIDE))
    for window in range(2):
        for cell in range(LENGTH):
            at = window * STRIDE + cell - RIM
            if at < 0:
                at = TILE + at + RIM
            elif at >= TILE:
                at = RIM + at
            across[at, window * LENGTH : (window + 1) * LENGTH] = tapered[:, cell]

    def low(array):
        return np.ascontiguousarray(array).astype(np.float32).astype(jnp.bfloat16)

    order = np.arange(LENGTH).reshape(2, 2, PIECE).transpose(1, 0, 2).reshape(-1)
    return low(across), low(across.T), low(tapered), low(tapered.T[:, order])


NEEDED = []
for _tx in (0, 1):
    for _ty in (0, 1):
        NEEDED += [(_tx, _ty, _dx, _dy) for _dx in (-1, 0, 1) for _dy in (-1, 0, 1)]
for _t in (0, 1):
    NEEDED += [(_t, -1, _dx, 1) for _dx in (-1, 0, 1)]
    NEEDED += [(_t, 2, _dx, -1) for _dx in (-1, 0, 1)]
    NEEDED += [(-1, _t, 1, _dy) for _dy in (-1, 0, 1)]
    NEEDED += [(2, _t, -1, _dy) for _dy in (-1, 0, 1)]
PLACE = {key: index for index, key in enumerate(NEEDED)}


def contract(left, right, left_dim, right_dim):
    return lax.dot_general(
        left, right, (((left_dim,), (right_dim,)), ((), ())), preferred_element_type=F32
    )


def selector(rows, columns, target):
    row = lax.broadcasted_iota(jnp.int32, (rows, columns), 0)
    column = lax.broadcasted_iota(jnp.int32, (rows, columns), 1)
    return jnp.where(column == target(row), 1.0, 0.0).astype(BF16)


def sine_cosine(angle):
    turns = jnp.floor(angle * np.float32(2 / np.pi) + 0.5)
    rest = angle - turns * np.float32(1.5703125)
    rest = rest - turns * np.float32(4.837512969970703e-4)
    rest = rest - turns * np.float32(7.549789954891882e-8)
    square = rest * rest
    sine = np.float32(-1.9515295891e-4) * square + np.float32(8.3321608736e-3)
    sine = sine * square + np.float32(-1.6666654611e-1)
    sine = sine * square * rest + rest
    cosine = np.float32(2.443315711809948e-5) * square + np.float32(-1.388731625493765e-3)
    cosine = cosine * square + np.float32(4.166664568298827e-2)
    cosine = cosine * square * square + (1.0 - 0.5 * square)
    quarter = turns.astype(jnp.int32)
    swap = (quarter & 1) != 0
    first = jnp.where(swap, cosine, sine)
    second = jnp.where(swap, sine, cosine)
    first = jnp.where((quarter & 2) != 0, -first, first)
    second = jnp.where(((quarter + 1) & 2) != 0, -second, second)
    return first, second


SIDES = (-1, 1)


def lands(step):
    return 0 if step > 0 else 1


def leaves(step):
    return 1 if step > 0 else 0


def kernel(
    sizes,
    x_hbm,
    slow_hbm,
    freq,
    prop_hbm,
    group_hbm,
    reach_hbm,
    coup_hbm,
    a1_hbm,
    b1_hbm,
    a2_hbm,
    b2_hbm,
    out_real,
    out_imag,
    xv,
    slow,
    big,
    a1,
    b1,
    a2,
    b2,
    hs,
    hr,
    xr,
    hc,
    fp32,
    fp,
    cf,
    swa,
    swb,
    ra,
    rb,
    pa,
    pb,
    qa,
    qb,
    acc,
    mixed,
    pg,
    second,
    canvas,
    cosv,
    sinv,
    ors,
    orr,
    ocs,
    ocr,
    occ,
    occr,
    group,
    reach,
    coup,
    weights,
    held,
    local_sem,
    send_sem,
    recv_sem,
    pass_send,
    pass_recv,
):
    size_x, size_y = sizes
    total_x = 2 * size_x
    total_y = 2 * size_y
    gx = lax.axis_index("gx")
    gy = lax.axis_index("gy")
    has = {
        ("gx", -1): gx > 0,
        ("gx", 1): gx < size_x - 1,
        ("gy", -1): gy > 0,
        ("gy", 1): gy < size_y - 1,
    }
    here = {"gx": gx, "gy": gy}
    ways = [{"gx": step} for step in SIDES] + [{"gy": step} for step in SIDES]
    ways += [{"gx": sx, "gy": sy} for sx in SIDES for sy in SIDES]

    def exists(way, sign=1):
        found = [has[axis, sign * step] for axis, step in way.items()]
        return found[0] if len(found) == 1 else jnp.logical_and(*found)

    def device(way):
        return {axis: here[axis] + step for axis, step in way.items()}

    half_x = size_x // 2
    relays = size_x % 2 == 0 and size_y % 4 == 0
    odd = lax.rem(gy, 2) == 1
    other = gy + 2 - 4 * lax.rem(lax.div(gy, 2), 2)
    leaving = {1: gx == half_x - 1, -1: gx == half_x}
    relayed = {step: jnp.logical_and(odd, leaving[step]) for step in SIDES}

    barrier = pltpu.get_barrier_semaphore()
    if relays:
        for step in SIDES:

            @pl.when(relayed[step])
            def _(step=step):
                for target in ({"gx": gx + step, "gy": other}, {"gy": other}):
                    pl.semaphore_signal(
                        barrier, inc=1, device_id=target, device_id_type=pl.DeviceIdType.MESH
                    )

    for way in ways:

        @pl.when(exists(way))
        def _(way=way):
            pl.semaphore_signal(
                barrier, inc=1, device_id=device(way), device_id_type=pl.DeviceIdType.MESH
            )

    base_x = jnp.clip(2 * gx - 1, 0, total_x - 4)
    copies = {
        "x0": [(x_hbm.at[0, 0], xv.at[0:TILE])],
        "x1": [(x_hbm.at[1, 0], xv.at[TILE:])],
        "a1": [(a1_hbm, a1)],
        "reach": [(reach_hbm, reach)],
        "coup": [(coup_hbm.at[pl.ds(base_x, 4)], coup)],
        "group": [(group_hbm, group)],
        "a2": [(a2_hbm, a2)],
    }
    for which in range(3):
        copies["real%d" % which] = [
            (prop_hbm.at[which, 0, 0], big.at[which, 0:LENGTH, 0:LENGTH]),
            (prop_hbm.at[which, 0, 0], big.at[which, LENGTH:WIDE, LENGTH:WIDE]),
            (prop_hbm.at[which, 0, 1], big.at[which, LENGTH:WIDE, 0:LENGTH]),
        ]
    copies["slow"] = [(slow_hbm, slow)]
    copies["b1"] = [(b1_hbm, b1)]
    copies["b2"] = [(b2_hbm, b2)]
    loads = {}
    number = 0
    for name, pairs in copies.items():
        loads[name] = []
        for source, target in pairs:
            loads[name].append(pltpu.make_async_copy(source, target, local_sem.at[number]))
            number += 1
    for batch in loads.values():
        for load in batch:
            load.start()

    def loaded(name):
        for load in loads[name]:
            load.wait()

    counter = [0]

    def message(way, source, target):
        counter[0] += 1
        return counter[0] - 1, way, source, target

    def copy_of(item):
        slot, way, source, target = item
        return pltpu.make_async_remote_copy(
            src_ref=source,
            dst_ref=target,
            send_sem=send_sem.at[slot],
            recv_sem=recv_sem.at[slot],
            device_id=device(way),
            device_id_type=pl.DeviceIdType.MESH,
        )

    def start(items):
        for item in items:

            @pl.when(exists(item[1]))
            def _(item=item):
                copy_of(item).start()

    def detour(item, place):
        slot, way, source, _ = item
        return pltpu.make_async_remote_copy(
            src_ref=source,
            dst_ref=held.at[place],
            send_sem=send_sem.at[slot],
            recv_sem=pass_recv.at[place],
            device_id={"gx": gx + way["gx"], "gy": other},
            device_id_type=pl.DeviceIdType.MESH,
        )

    def onward(item, place):
        slot, _, _, target = item
        return pltpu.make_async_remote_copy(
            src_ref=held.at[place],
            dst_ref=target,
            send_sem=pass_send.at[place],
            recv_sem=recv_sem.at[slot],
            device_id={"gy": other},
            device_id_type=pl.DeviceIdType.MESH,
        )

    def start_long(items, place):
        if not relays:
            start(items)
            return
        for item in items:
            step = item[1]["gx"]

            @pl.when(jnp.logical_and(exists(item[1]), jnp.logical_not(relayed[step])))
            def _(item=item):
                copy_of(item).start()

            @pl.when(relayed[step])
            def _(item=item):
                detour(item, place).start()

    def pass_on(items, place):
        if not relays:
            return
        for item in items:

            @pl.when(relayed[-item[1]["gx"]])
            def _(item=item):
                detour(item, place).wait_recv()
                onward(item, place).start()

    def passed(items, place):
        if not relays:
            return
        for item in items:

            @pl.when(relayed[-item[1]["gx"]])
            def _(item=item):
                onward(item, place).wait_send()

    def arrive(items):
        for item in items:

            @pl.when(exists(item[1], -1))
            def _(item=item):
                copy_of(item).wait_recv()

    def drain(items):
        for item in items:

            @pl.when(exists(item[1]))
            def _(item=item):
                copy_of(item).wait_send()

    def clear_missing(items):
        for item in items:

            @pl.when(jnp.logical_not(exists(item[1], -1)))
            def _(target=item[3]):
                target[...] = jnp.zeros(target.shape, target.dtype)

    row_rims = [
        message({"gx": -1}, x_hbm.at[:, 0, 0:RIM], xr.at[1]),
        message({"gx": 1}, x_hbm.at[:, 0, TILE - RIM : TILE], xr.at[0]),
    ]
    column_rims = [message({"gy": step}, hs.at[leaves(step)], hr.at[lands(step)]) for step in SIDES]
    corner_rims = [
        message(
            {"gx": sx, "gy": sy},
            hs.at[leaves(sy), :, :, 0:128] if sx < 0 else hs.at[leaves(sy), :, :, 384:512],
            hc.at[lands(sx), lands(sy)],
        )
        for sx in SIDES
        for sy in SIDES
    ]

    def sided(axis, piece, source, target):
        return [
            message({axis: step}, source.at[piece, leaves(step)], target.at[piece, lands(step)])
            for step in SIDES
        ]

    a_items = [sided("gx", piece, swa, ra) for piece in range(2)]
    b_items = [sided("gy", piece, swb, rb) for piece in range(2)]
    pa_items = [sided("gy", piece, pa, qa) for piece in range(2)]
    pb_items = [sided("gx", piece, pb, qb) for piece in range(2)]
    row_sums = [message({"gx": step}, ors.at[leaves(step)], orr.at[lands(step)]) for step in SIDES]
    column_sums = [message({"gy": step}, ocs.at[leaves(step)], ocr.at[lands(step)]) for step in SIDES]
    corner_sums = [
        message({"gx": sx, "gy": sy}, occ.at[leaves(sx)], occr.at[lands(sx), lands(sy)])
        for sx in SIDES
        for sy in SIDES
    ]

    pick = selector(OVER, TILE, lambda r: jnp.where(r < RIM, r, r + TILE - OVER))
    hs[:, :, :, 384:512] = jnp.zeros((2, 2, RIM, 128), BF16)
    for part in range(2):
        loaded("x%d" % part)
        rims = contract(pick, xv[part * TILE : (part + 1) * TILE], 1, 1).astype(BF16)
        hs[0, part, :, 0:TILE] = rims[:RIM]
        hs[1, part, :, 0:TILE] = rims[RIM:]
    for items in (row_rims, column_rims, corner_rims, row_sums, column_sums, corner_sums):
        clear_missing(items)
    expected = sum(exists(way).astype(jnp.int32) for way in ways)
    if relays:
        expected = expected + sum(2 * relayed[step].astype(jnp.int32) for step in SIDES)
    pl.semaphore_wait(barrier, expected)
    start(corner_rims)
    start(column_rims)
    start(row_rims)

    loaded("a1")
    fp32[...] = jnp.dot(xv[...], a1[:TILE], preferred_element_type=F32)

    loaded("reach")
    loaded("coup")
    for tx, ty in sorted({key[:2] for key in NEEDED}):
        at_x = 2 * gx + tx
        at_y = 2 * gy + ty
        near_x = jnp.clip(at_x, 0, total_x - 1)
        near_y = jnp.clip(at_y, 0, total_y - 1)
        row = near_x - base_x
        slots = [
            (reach[s, near_x, near_y], coup[row, s, 0, near_y], coup[row, s, 1, near_y])
            for s in range(reach.shape[0])
        ]
        for key, place in PLACE.items():
            if key[:2] != (tx, ty):
                continue
            window = (at_x + key[2]) * total_y + at_y + key[3]
            window = jnp.where(at_x + key[2] < 0, -2, window)
            real = jnp.float32(0.0)
            imag = jnp.float32(0.0)
            for entry, entry_real, entry_imag in slots:
                same = entry == window
                real = jnp.where(same, entry_real, real)
                imag = jnp.where(same, entry_imag, imag)
            weights[2 * place] = real
            weights[2 * place + 1] = imag
    for which in range(3):
        loaded("real%d" % which)
        big[which, 0:LENGTH, LENGTH:WIDE] = -big[which, LENGTH:WIDE, 0:LENGTH]
    loaded("a2")
    loaded("group")
    for piece in range(2):
        clear_missing(a_items[piece])
        clear_missing(b_items[piece])

    a1_rims = a1[TILE : TILE + OVER]
    arrive(column_rims)
    for part in range(2):
        rims = jnp.concatenate([hr[0, part, :, 0:TILE], hr[1, part, :, 0:TILE]], axis=0)
        fp[part, RIM : TILE + RIM] = (
            fp32[part * TILE : (part + 1) * TILE] + contract(rims, a1_rims, 0, 0)
        ).astype(BF16)
    arrive(row_rims)
    arrive(corner_rims)
    beyond = jnp.dot(xr[...].reshape(4 * RIM, TILE), a1[:TILE], preferred_element_type=F32)
    for side in range(2):
        corners = jnp.concatenate(
            [
                jnp.concatenate([hc[side, 0, part], hc[side, 1, part]], axis=0)
                for part in range(2)
            ],
            axis=1,
        )
        corners = contract(corners, a1_rims, 0, 0)
        skip = 48 if side == 0 else 0
        to = 0 if side == 0 else TILE + RIM
        for part in range(2):
            at = (2 * side + part) * RIM
            fp[part, to : to + RIM] = (
                beyond[at : at + RIM] + corners[part * 128 + skip : part * 128 + skip + RIM]
            ).astype(BF16)

    for wx in range(2):
        for part in range(2):
            found = jnp.dot(
                a2[...],
                fp[part, wx * STRIDE : wx * STRIDE + LENGTH],
                preferred_element_type=F32,
            ).astype(BF16)
            for wy in range(2):
                cf[wx, wy, part * LENGTH : (part + 1) * LENGTH] = found[
                    :, wy * LENGTH : (wy + 1) * LENGTH
                ]

    def group_of(wx, wy):
        return group[2 * gx + wx, 2 * gy + wy]

    for wx in range(2):
        for wy in range(2):
            swept = jnp.dot(
                big[group_of(wx, wy)], cf[wx, wy], preferred_element_type=F32
            ).astype(BF16)
            for part in range(2):
                for piece in range(2):
                    at = part * LENGTH + piece * PIECE
                    swa[piece, wx, wy, part] = swept[at : at + PIECE]
                    at = at + 2 * PIECE
                    swb[piece, wy, wx, part] = swept[at : at + PIECE]
        if wx == 0:
            start_long([a_items[0][0]], 0)
    start_long([a_items[0][1]], 0)
    start(b_items[0])
    start_long(a_items[1], 1)
    start(b_items[1])

    def source(half, piece, x, y):
        if half == 0:
            if x in (0, 1):
                return swa.at[piece, x, y]
            return ra.at[piece, 0 if x < 0 else 1, y]
        if y in (0, 1):
            return swb.at[piece, y, x]
        return rb.at[piece, 0 if y < 0 else 1, x]

    def rows(chunk, start=0):
        return pl.ds(pl.multiple_of(start + chunk * CHUNK, CHUNK), CHUNK)

    def mix(half, piece, sums, get, put):
        def body(chunk, carry):
            at = rows(chunk)
            held = {}

            def value(x, y):
                if (x, y) not in held:
                    ref = source(half, piece, x, y)
                    held[x, y] = (ref[0, at, :].astype(F32), ref[1, at, :].astype(F32))
                return held[x, y]

            for (tx, ty), sources in sums:
                real, imag = get(tx, ty, at) if get is not None else (None, None)
                for sx, sy in sources:
                    place = PLACE[tx, ty, sx - tx, sy - ty]
                    w_real = weights[2 * place]
                    w_imag = weights[2 * place + 1]
                    v_real, v_imag = value(sx, sy)
                    add_real = w_real * v_real - w_imag * v_imag
                    add_imag = w_real * v_imag + w_imag * v_real
                    real = add_real if real is None else real + add_real
                    imag = add_imag if imag is None else imag + add_imag
                put(tx, ty, at, real, imag)
            return carry

        lax.fori_loop(0, PIECE // CHUNK, body, 0)

    def acc_get(half, piece):
        def get(tx, ty, at):
            return acc[half, piece, tx, ty, 0, at, :], acc[half, piece, tx, ty, 1, at, :]

        return get

    def acc_put(half, piece):
        def put(tx, ty, at, real, imag):
            acc[half, piece, tx, ty, 0, at, :] = real
            acc[half, piece, tx, ty, 1, at, :] = imag

        return put

    inner = [(x, y) for x in (0, 1) for y in (0, 1)]
    for piece in range(2):
        for half in range(2):
            mix(half, piece, [(target, inner) for target in inner], None, acc_put(half, piece))
        clear_missing(pa_items[piece])
        clear_missing(pb_items[piece])

    loaded("slow")

    def phase_rows(chunk, carry):
        at = rows(chunk)
        sinv[at, :], cosv[at, :] = sine_cosine(freq[0] * slow[at, :])
        return carry

    lax.fori_loop(0, TILE // CHUNK, phase_rows, 0)

    def pa_put(piece):
        def put(tx, ty, at, real, imag):
            side = 0 if ty < 0 else 1
            pa[piece, side, tx, 0, at, :] = real.astype(BF16)
            pa[piece, side, tx, 1, at, :] = imag.astype(BF16)

        return put

    def pb_put(piece):
        def put(tx, ty, at, real, imag):
            side = 0 if tx < 0 else 1
            pb[piece, side, ty, 0, at, :] = real.astype(BF16)
            pb[piece, side, ty, 1, at, :] = imag.astype(BF16)

        return put

    near = (-1, 0, 1)

    def sums_along_y(piece):
        arrive(a_items[piece])
        mix(
            0,
            piece,
            [((t, -1), [(t + d, 0) for d in near]) for t in (0, 1)]
            + [((t, 2), [(t + d, 1) for d in near]) for t in (0, 1)],
            None,
            pa_put(piece),
        )
        start(pa_items[piece])

    def sums_along_x(piece):
        arrive(b_items[piece])
        mix(
            1,
            piece,
            [((-1, t), [(0, t + d) for d in near]) for t in (0, 1)]
            + [((2, t), [(1, t + d) for d in near]) for t in (0, 1)],
            None,
            pb_put(piece),
        )
        start_long(pb_items[piece], 2 + piece)

    def add_along_x(piece):
        mix(
            0,
            piece,
            [((0, y), [(-1, 0), (-1, 1)]) for y in (0, 1)]
            + [((1, y), [(2, 0), (2, 1)]) for y in (0, 1)],
            acc_get(0, piece),
            acc_put(0, piece),
        )

    def add_along_y(piece):
        mix(
            1,
            piece,
            [((x, 0), [(0, -1), (1, -1)]) for x in (0, 1)]
            + [((x, 1), [(0, 2), (1, 2)]) for x in (0, 1)],
            acc_get(1, piece),
            acc_put(1, piece),
        )

    pass_on(a_items[0], 0)
    sums_along_x(0)
    pass_on(a_items[1], 1)
    sums_along_x(1)
    sums_along_y(0)
    add_along_y(0)
    add_along_y(1)
    pass_on(pb_items[0], 2)
    sums_along_y(1)
    add_along_x(0)
    pass_on(pb_items[1], 3)
    add_along_x(1)
    loaded("b1")
    loaded("b2")

    span = 2 * PIECE
    for piece in range(2):
        arrive(pa_items[piece])
        arrive(pb_items[piece])

        def join(chunk, carry, piece=piece):
            at = rows(chunk)
            below = rows(chunk, PIECE)
            for tx, ty in inner:
                for part in range(2):
                    lanes = slice(part * LENGTH, (part + 1) * LENGTH)
                    mixed[piece, tx, ty, at, lanes] = (
                        acc[0, piece, tx, ty, part, at, :]
                        + qa[piece, ty, tx, part, at, :].astype(F32)
                    ).astype(BF16)
                    mixed[piece, tx, ty, below, lanes] = (
                        acc[1, piece, tx, ty, part, at, :]
                        + qb[piece, tx, ty, part, at, :].astype(F32)
                    ).astype(BF16)
            return carry

        lax.fori_loop(0, PIECE // CHUNK, join, 0)
        for wx in range(2):
            for wy in range(2):
                spread = contract(mixed[piece, wx, wy], big[group_of(wx, wy)], 1, 1).astype(BF16)
                for part in range(2):
                    at = (2 * wx + part) * span
                    pg[piece, at : at + span, wy * LENGTH : (wy + 1) * LENGTH] = spread[
                        :, part * LENGTH : (part + 1) * LENGTH
                    ]
        across = jnp.dot(pg[piece], b1[...], preferred_element_type=F32).astype(BF16)
        for wx in range(2):
            for part in range(2):
                at = (2 * wx + part) * span
                second[wx, part, piece * span : (piece + 1) * span] = across[at : at + span]

    for part in range(2):
        pieces = [
            jnp.dot(b2[...], second[wx, part], preferred_element_type=F32) for wx in range(2)
        ]
        canvas[part, 0:STRIDE] = pieces[0][:STRIDE]
        canvas[part, STRIDE:LENGTH] = pieces[0][STRIDE:] + pieces[1][:OVER]
        canvas[part, LENGTH : TILE + OVER] = pieces[1][OVER:]
    own = slice(RIM, TILE + RIM)
    ends = (slice(0, RIM), slice(TILE + RIM, TILE + OVER))
    for side in range(2):
        ors[side] = canvas[:, ends[side], 0:TILE].astype(BF16)
        occ[side] = canvas[:, ends[side], 384:512].astype(BF16)
    start(corner_sums)
    start(row_sums)
    pick_rim = selector(OVER, 128, lambda r: r + 64)
    for part in range(2):
        rims = contract(pick_rim, canvas[part, own, 384:512].astype(BF16), 1, 1).astype(BF16)
        ocs[0, part] = rims[:RIM]
        ocs[1, part] = rims[RIM:]
    start(column_sums)
    first = selector(RIM, 128, lambda r: r)
    last = selector(RIM, 128, lambda r: r + 48)
    edges = (slice(RIM, 2 * RIM), slice(TILE, TILE + RIM))
    lane = lax.broadcasted_iota(jnp.int32, (128, 128), 0)
    to = lax.broadcasted_iota(jnp.int32, (128, 128), 1)
    first_corner = jnp.where((to < RIM) & (lane == to + 80), 1.0, 0.0).astype(BF16)
    last_corner = jnp.where((to >= 48) & (to < 64) & (lane == to + 16), 1.0, 0.0).astype(BF16)
    def finish_rows(chunk, lanes):
        at = rows(chunk)
        inside = rows(chunk, RIM)
        real = canvas[0, inside, lanes]
        imag = canvas[1, inside, lanes]
        cosine = cosv[at, lanes]
        sine = sinv[at, lanes]
        out_real[at, lanes] = (real * cosine - imag * sine).astype(BF16)
        out_imag[at, lanes] = (real * sine + imag * cosine).astype(BF16)

    middle = slice(128, 384)
    final = TILE // CHUNK - 1

    def finish_middle(chunk, carry):
        finish_rows(chunk, middle)
        return carry

    lax.fori_loop(1, final, finish_middle, 0)
    arrive(row_sums)
    for side in range(2):
        canvas[:, edges[side], 0:TILE] = canvas[:, edges[side], 0:TILE] + orr[side].astype(F32)
        finish_rows(side * final, middle)
    arrive(column_sums)
    for part in range(2):
        canvas[part, own, 0:128] = canvas[part, own, 0:128] + contract(ocr[0, part], first, 0, 0)
        canvas[part, own, 384:512] = canvas[part, own, 384:512] + contract(ocr[1, part], last, 0, 0)

    def finish_sides(chunk, carry):
        finish_rows(chunk, slice(0, 128))
        finish_rows(chunk, slice(384, TILE))
        return carry

    lax.fori_loop(1, final, finish_sides, 0)
    arrive(corner_sums)
    for side in range(2):
        for part in range(2):
            canvas[part, edges[side], 0:128] = canvas[part, edges[side], 0:128] + contract(
                occr[side, 0, part], first_corner, 1, 0
            )
            canvas[part, edges[side], 384:512] = canvas[part, edges[side], 384:512] + contract(
                occr[side, 1, part], last_corner, 1, 0
            )
        finish_sides(side * final, 0)
    for items in [row_rims, column_rims, corner_rims, row_sums, column_sums, corner_sums]:
        drain(items)
    for piece in range(2):
        for items in (a_items, b_items, pa_items, pb_items):
            drain(items[piece])
        passed(a_items[piece], piece)
        passed(pb_items[piece], 2 + piece)


def per_device(
    sizes, wavefield, slowness, frequencies, propagator, window_velocity_group, reach_list, coupling
):
    a1, b1, a2, b2 = (jnp.asarray(table) for table in tables())
    anywhere = pl.BlockSpec(memory_space=pl.ANY)
    vmem = pltpu.VMEM
    pieces = (2, 2, 2, 2, PIECE, LENGTH)
    groups, slots = propagator.shape[0], reach_list.shape[2]
    call = pl.pallas_call(
        functools.partial(kernel, sizes),
        out_shape=[jax.ShapeDtypeStruct((TILE, TILE), BF16)] * 2,
        in_specs=[anywhere, anywhere, pl.BlockSpec(memory_space=pltpu.SMEM)] + [anywhere] * 8,
        out_specs=[pl.BlockSpec(memory_space=pltpu.VMEM)] * 2,
        scratch_shapes=[
            vmem((2 * TILE, TILE), BF16),
            vmem((TILE, TILE), F32),
            vmem((groups, WIDE, WIDE), BF16),
            vmem((WIDE, WIDE), BF16),
            vmem((WIDE, WIDE), BF16),
            vmem((LENGTH, LENGTH), BF16),
            vmem((LENGTH, LENGTH), BF16),
            vmem((2, 2, RIM, WIDE), BF16),
            vmem((2, 2, RIM, WIDE), BF16),
            vmem((2, 2, RIM, TILE), BF16),
            vmem((2, 2, 2, RIM, 128), BF16),
            vmem((2 * TILE, WIDE), F32),
            vmem((2, TILE + OVER, WIDE), BF16),
            vmem((2, 2, WIDE, LENGTH), BF16),
        ]
        + [vmem(pieces, BF16)] * 8
        + [
            vmem((2, 2, 2, 2, 2, PIECE, LENGTH), F32),
            vmem((2, 2, 2, 2 * PIECE, WIDE), BF16),
            vmem((2, 8 * PIECE, WIDE), BF16),
            vmem((2, 2, LENGTH, WIDE), BF16),
            vmem((2, TILE + OVER, WIDE), F32),
            vmem((TILE, TILE), F32),
            vmem((TILE, TILE), F32),
            vmem((2, 2, RIM, TILE), BF16),
            vmem((2, 2, RIM, TILE), BF16),
            vmem((2, 2, RIM, TILE), BF16),
            vmem((2, 2, RIM, TILE), BF16),
            vmem((2, 2, RIM, 128), BF16),
            vmem((2, 2, 2, RIM, 128), BF16),
            pltpu.SMEM(window_velocity_group.shape, jnp.int32),
            pltpu.SMEM((slots, *reach_list.shape[:2]), jnp.int32),
            pltpu.SMEM((4, slots, 2, coupling.shape[1]), F32),
            pltpu.SMEM((2 * len(NEEDED),), F32),
            vmem((4, 2, 2, PIECE, LENGTH), BF16),
            pltpu.SemaphoreType.DMA((19,)),
            pltpu.SemaphoreType.DMA((32,)),
            pltpu.SemaphoreType.DMA((32,)),
            pltpu.SemaphoreType.DMA((4,)),
            pltpu.SemaphoreType.DMA((4,)),
        ],
        compiler_params=pltpu.CompilerParams(
            collective_id=0, has_side_effects=True, vmem_limit_bytes=60 * 1024 * 1024
        ),
    )
    parts = call(
        wavefield,
        slowness,
        frequencies,
        propagator,
        window_velocity_group,
        jnp.transpose(reach_list, (2, 0, 1)),
        jnp.transpose(coupling, (0, 2, 3, 1)),
        a1,
        b1,
        a2,
        b2,
    )
    return jnp.stack(parts)[:, None]


def solution(mesh):
    sizes = (mesh.shape["gx"], mesh.shape["gy"])
    return jax.shard_map(
        functools.partial(per_device, sizes),
        mesh=mesh,
        in_specs=(P(None, None, "gx", "gy"), P("gx", "gy"), P(), P(), P(), P(), P()),
        out_specs=P(None, None, "gx", "gy"),
        check_vma=False,
    )
```

```python
import functools

import jax
import jax.numpy as jnp
import numpy as np
from jax import lax
from jax.experimental import pallas as pl
from jax.experimental.pallas import tpu as pltpu
from jax.sharding import PartitionSpec as P

LENGTH = 256
OVER = 32
RIM = OVER // 2
STRIDE = LENGTH - OVER
TILE = 2 * STRIDE
WIDE = 2 * LENGTH
PIECE = LENGTH // 4
CHUNK = 16
BF16 = jnp.bfloat16
F32 = jnp.float32


def tables():
    points = np.arange(LENGTH) + 0.5
    cosines = np.sqrt(2.0 / LENGTH) * np.cos(np.pi / LENGTH * points[:, None] * points[None, :])
    cosines = cosines.astype(np.float32).astype(jnp.bfloat16).astype(np.float64)
    cells = np.arange(LENGTH)
    rising = np.sin(0.5 * np.pi * (cells + 0.5) / OVER)
    falling = np.cos(0.5 * np.pi * (cells - STRIDE + 0.5) / OVER)
    bell = np.where(cells < OVER, rising, np.where(cells >= STRIDE, falling, 1.0))
    tapered = cosines * bell[None, :]
    across = np.zeros((WIDE, WIDE))
    for window in range(2):
        for cell in range(LENGTH):
            at = window * STRIDE + cell - RIM
            if at < 0:
                at = TILE + at + RIM
            elif at >= TILE:
                at = RIM + at
            across[at, window * LENGTH : (window + 1) * LENGTH] = tapered[:, cell]

    def low(array):
        return np.ascontiguousarray(array).astype(np.float32).astype(jnp.bfloat16)

    order = np.arange(LENGTH).reshape(2, 2, PIECE).transpose(1, 0, 2).reshape(-1)
    return low(across), low(across.T), low(tapered), low(tapered.T[:, order])


NEEDED = []
for _tx in (0, 1):
    for _ty in (0, 1):
        NEEDED += [(_tx, _ty, _dx, _dy) for _dx in (-1, 0, 1) for _dy in (-1, 0, 1)]
for _t in (0, 1):
    NEEDED += [(_t, -1, _dx, 1) for _dx in (-1, 0, 1)]
    NEEDED += [(_t, 2, _dx, -1) for _dx in (-1, 0, 1)]
    NEEDED += [(-1, _t, 1, _dy) for _dy in (-1, 0, 1)]
    NEEDED += [(2, _t, -1, _dy) for _dy in (-1, 0, 1)]
PLACE = {key: index for index, key in enumerate(NEEDED)}


def contract(left, right, left_dim, right_dim):
    return lax.dot_general(
        left, right, (((left_dim,), (right_dim,)), ((), ())), preferred_element_type=F32
    )


def selector(rows, columns, target):
    row = lax.broadcasted_iota(jnp.int32, (rows, columns), 0)
    column = lax.broadcasted_iota(jnp.int32, (rows, columns), 1)
    return jnp.where(column == target(row), 1.0, 0.0).astype(BF16)


def sine_cosine(angle):
    turns = jnp.floor(angle * np.float32(2 / np.pi) + 0.5)
    rest = angle - turns * np.float32(1.5703125)
    rest = rest - turns * np.float32(4.837512969970703e-4)
    rest = rest - turns * np.float32(7.549789954891882e-8)
    square = rest * rest
    sine = np.float32(-1.9515295891e-4) * square + np.float32(8.3321608736e-3)
    sine = sine * square + np.float32(-1.6666654611e-1)
    sine = sine * square * rest + rest
    cosine = np.float32(2.443315711809948e-5) * square + np.float32(-1.388731625493765e-3)
    cosine = cosine * square + np.float32(4.166664568298827e-2)
    cosine = cosine * square * square + (1.0 - 0.5 * square)
    quarter = turns.astype(jnp.int32)
    swap = (quarter & 1) != 0
    first = jnp.where(swap, cosine, sine)
    second = jnp.where(swap, sine, cosine)
    first = jnp.where((quarter & 2) != 0, -first, first)
    second = jnp.where(((quarter + 1) & 2) != 0, -second, second)
    return first, second


SIDES = (-1, 1)


def lands(step):
    return 0 if step > 0 else 1


def leaves(step):
    return 1 if step > 0 else 0


def kernel(
    sizes,
    x_hbm,
    slow_hbm,
    freq,
    prop_hbm,
    group_hbm,
    reach_hbm,
    coup_hbm,
    a1_hbm,
    b1_hbm,
    a2_hbm,
    b2_hbm,
    out_real,
    out_imag,
    xv,
    slow,
    big,
    a1,
    b1,
    a2,
    b2,
    hs,
    hr,
    xr,
    hc,
    fp32,
    fp,
    cf,
    swa,
    swb,
    ra,
    rb,
    pa,
    pb,
    qa,
    qb,
    acc,
    mixed,
    pg,
    second,
    canvas,
    cosv,
    sinv,
    ors,
    orr,
    ocs,
    ocr,
    occ,
    occr,
    group,
    reach,
    coup,
    weights,
    held,
    local_sem,
    send_sem,
    recv_sem,
    pass_send,
    pass_recv,
):
    size_x, size_y = sizes
    total_x = 2 * size_x
    total_y = 2 * size_y
    gx = lax.axis_index("gx")
    gy = lax.axis_index("gy")
    has = {
        ("gx", -1): gx > 0,
        ("gx", 1): gx < size_x - 1,
        ("gy", -1): gy > 0,
        ("gy", 1): gy < size_y - 1,
    }
    here = {"gx": gx, "gy": gy}
    ways = [{"gx": step} for step in SIDES] + [{"gy": step} for step in SIDES]
    ways += [{"gx": sx, "gy": sy} for sx in SIDES for sy in SIDES]

    def exists(way, sign=1):
        found = [has[axis, sign * step] for axis, step in way.items()]
        return found[0] if len(found) == 1 else jnp.logical_and(*found)

    def device(way):
        return {axis: here[axis] + step for axis, step in way.items()}

    half_x = size_x // 2
    relays = size_x % 2 == 0 and size_y % 4 == 0
    odd = lax.rem(gy, 2) == 1
    other = gy + 2 - 4 * lax.rem(lax.div(gy, 2), 2)
    leaving = {1: gx == half_x - 1, -1: gx == half_x}
    relayed = {step: jnp.logical_and(odd, leaving[step]) for step in SIDES}

    barrier = pltpu.get_barrier_semaphore()
    if relays:
        for step in SIDES:

            @pl.when(relayed[step])
            def _(step=step):
                for target in ({"gx": gx + step, "gy": other}, {"gy": other}):
                    pl.semaphore_signal(
                        barrier, inc=1, device_id=target, device_id_type=pl.DeviceIdType.MESH
                    )

    for way in ways:

        @pl.when(exists(way))
        def _(way=way):
            pl.semaphore_signal(
                barrier, inc=1, device_id=device(way), device_id_type=pl.DeviceIdType.MESH
            )

    base_x = jnp.clip(2 * gx - 1, 0, total_x - 4)
    copies = {
        "x0": [(x_hbm.at[0, 0], xv.at[0:TILE])],
        "x1": [(x_hbm.at[1, 0], xv.at[TILE:])],
        "a1": [(a1_hbm, a1)],
        "reach": [(reach_hbm, reach)],
        "coup": [(coup_hbm.at[pl.ds(base_x, 4)], coup)],
        "group": [(group_hbm, group)],
        "a2": [(a2_hbm, a2)],
    }
    for which in range(3):
        copies["real%d" % which] = [
            (prop_hbm.at[which, 0, 0], big.at[which, 0:LENGTH, 0:LENGTH]),
            (prop_hbm.at[which, 0, 0], big.at[which, LENGTH:WIDE, LENGTH:WIDE]),
            (prop_hbm.at[which, 0, 1], big.at[which, LENGTH:WIDE, 0:LENGTH]),
        ]
    copies["slow"] = [(slow_hbm, slow)]
    copies["b1"] = [(b1_hbm, b1)]
    copies["b2"] = [(b2_hbm, b2)]
    loads = {}
    number = 0
    for name, pairs in copies.items():
        loads[name] = []
        for source, target in pairs:
            loads[name].append(pltpu.make_async_copy(source, target, local_sem.at[number]))
            number += 1
    for batch in loads.values():
        for load in batch:
            load.start()

    def loaded(name):
        for load in loads[name]:
            load.wait()

    counter = [0]

    def message(way, source, target):
        counter[0] += 1
        return counter[0] - 1, way, source, target

    def copy_of(item):
        slot, way, source, target = item
        return pltpu.make_async_remote_copy(
            src_ref=source,
            dst_ref=target,
            send_sem=send_sem.at[slot],
            recv_sem=recv_sem.at[slot],
            device_id=device(way),
            device_id_type=pl.DeviceIdType.MESH,
        )

    def start(items):
        for item in items:

            @pl.when(exists(item[1]))
            def _(item=item):
                copy_of(item).start()

    def detour(item, place):
        slot, way, source, _ = item
        return pltpu.make_async_remote_copy(
            src_ref=source,
            dst_ref=held.at[place],
            send_sem=send_sem.at[slot],
            recv_sem=pass_recv.at[place],
            device_id={"gx": gx + way["gx"], "gy": other},
            device_id_type=pl.DeviceIdType.MESH,
        )

    def onward(item, place):
        slot, _, _, target = item
        return pltpu.make_async_remote_copy(
            src_ref=held.at[place],
            dst_ref=target,
            send_sem=pass_send.at[place],
            recv_sem=recv_sem.at[slot],
            device_id={"gy": other},
            device_id_type=pl.DeviceIdType.MESH,
        )

    def start_long(items, place):
        if not relays:
            start(items)
            return
        for item in items:
            step = item[1]["gx"]

            @pl.when(jnp.logical_and(exists(item[1]), jnp.logical_not(relayed[step])))
            def _(item=item):
                copy_of(item).start()

            @pl.when(relayed[step])
            def _(item=item):
                detour(item, place).start()

    def pass_on(items, place):
        if not relays:
            return
        for item in items:

            @pl.when(relayed[-item[1]["gx"]])
            def _(item=item):
                detour(item, place).wait_recv()
                onward(item, place).start()

    def passed(items, place):
        if not relays:
            return
        for item in items:

            @pl.when(relayed[-item[1]["gx"]])
            def _(item=item):
                onward(item, place).wait_send()

    def arrive(items):
        for item in items:

            @pl.when(exists(item[1], -1))
            def _(item=item):
                copy_of(item).wait_recv()

    def drain(items):
        for item in items:

            @pl.when(exists(item[1]))
            def _(item=item):
                copy_of(item).wait_send()

    def clear_missing(items):
        for item in items:

            @pl.when(jnp.logical_not(exists(item[1], -1)))
            def _(target=item[3]):
                target[...] = jnp.zeros(target.shape, target.dtype)

    row_rims = [
        message({"gx": -1}, x_hbm.at[:, 0, 0:RIM], xr.at[1]),
        message({"gx": 1}, x_hbm.at[:, 0, TILE - RIM : TILE], xr.at[0]),
    ]
    column_rims = [message({"gy": step}, hs.at[leaves(step)], hr.at[lands(step)]) for step in SIDES]
    corner_rims = [
        message(
            {"gx": sx, "gy": sy},
            hs.at[leaves(sy), :, :, 0:128] if sx < 0 else hs.at[leaves(sy), :, :, 384:512],
            hc.at[lands(sx), lands(sy)],
        )
        for sx in SIDES
        for sy in SIDES
    ]

    def sided(axis, piece, source, target):
        return [
            message({axis: step}, source.at[piece, leaves(step)], target.at[piece, lands(step)])
            for step in SIDES
        ]

    a_items = [sided("gx", piece, swa, ra) for piece in range(2)]
    b_items = [sided("gy", piece, swb, rb) for piece in range(2)]
    pa_items = [sided("gy", piece, pa, qa) for piece in range(2)]
    pb_items = [sided("gx", piece, pb, qb) for piece in range(2)]
    row_sums = [message({"gx": step}, ors.at[leaves(step)], orr.at[lands(step)]) for step in SIDES]
    column_sums = [message({"gy": step}, ocs.at[leaves(step)], ocr.at[lands(step)]) for step in SIDES]
    corner_sums = [
        message({"gx": sx, "gy": sy}, occ.at[leaves(sx)], occr.at[lands(sx), lands(sy)])
        for sx in SIDES
        for sy in SIDES
    ]

    pick = selector(OVER, TILE, lambda r: jnp.where(r < RIM, r, r + TILE - OVER))
    hs[:, :, :, 384:512] = jnp.zeros((2, 2, RIM, 128), BF16)
    for part in range(2):
        loaded("x%d" % part)
        rims = contract(pick, xv[part * TILE : (part + 1) * TILE], 1, 1).astype(BF16)
        hs[0, part, :, 0:TILE] = rims[:RIM]
        hs[1, part, :, 0:TILE] = rims[RIM:]
    for items in (row_rims, column_rims, corner_rims, row_sums, column_sums, corner_sums):
        clear_missing(items)
    expected = sum(exists(way).astype(jnp.int32) for way in ways)
    if relays:
        expected = expected + sum(2 * relayed[step].astype(jnp.int32) for step in SIDES)
    pl.semaphore_wait(barrier, expected)
    start(corner_rims)
    start(column_rims)
    start(row_rims)

    loaded("a1")
    fp32[...] = jnp.dot(xv[...], a1[:TILE], preferred_element_type=F32)

    loaded("reach")
    loaded("coup")
    for tx, ty in sorted({key[:2] for key in NEEDED}):
        at_x = 2 * gx + tx
        at_y = 2 * gy + ty
        near_x = jnp.clip(at_x, 0, total_x - 1)
        near_y = jnp.clip(at_y, 0, total_y - 1)
        row = near_x - base_x
        slots = [
            (reach[s, near_x, near_y], coup[row, s, 0, near_y], coup[row, s, 1, near_y])
            for s in range(reach.shape[0])
        ]
        for key, place in PLACE.items():
            if key[:2] != (tx, ty):
                continue
            window = (at_x + key[2]) * total_y + at_y + key[3]
            window = jnp.where(at_x + key[2] < 0, -2, window)
            real = jnp.float32(0.0)
            imag = jnp.float32(0.0)
            for entry, entry_real, entry_imag in slots:
                same = entry == window
                real = jnp.where(same, entry_real, real)
                imag = jnp.where(same, entry_imag, imag)
            weights[2 * place] = real
            weights[2 * place + 1] = imag
    for which in range(3):
        loaded("real%d" % which)
        big[which, 0:LENGTH, LENGTH:WIDE] = -big[which, LENGTH:WIDE, 0:LENGTH]
    loaded("a2")
    loaded("group")
    for piece in range(2):
        clear_missing(a_items[piece])
        clear_missing(b_items[piece])

    a1_rims = a1[TILE : TILE + OVER]
    arrive(column_rims)
    for part in range(2):
        rims = jnp.concatenate([hr[0, part, :, 0:TILE], hr[1, part, :, 0:TILE]], axis=0)
        fp[part, RIM : TILE + RIM] = (
            fp32[part * TILE : (part + 1) * TILE] + contract(rims, a1_rims, 0, 0)
        ).astype(BF16)
    arrive(row_rims)
    beyond = jnp.dot(xr[...].reshape(4 * RIM, TILE), a1[:TILE], preferred_element_type=F32)
    arrive(corner_rims)
    for side in range(2):
        corners = jnp.concatenate(
            [
                jnp.concatenate([hc[side, 0, part], hc[side, 1, part]], axis=0)
                for part in range(2)
            ],
            axis=1,
        )
        corners = contract(corners, a1_rims, 0, 0)
        skip = 48 if side == 0 else 0
        to = 0 if side == 0 else TILE + RIM
        for part in range(2):
            at = (2 * side + part) * RIM
            fp[part, to : to + RIM] = (
                beyond[at : at + RIM] + corners[part * 128 + skip : part * 128 + skip + RIM]
            ).astype(BF16)

    for wx in range(2):
        for part in range(2):
            found = jnp.dot(
                a2[...],
                fp[part, wx * STRIDE : wx * STRIDE + LENGTH],
                preferred_element_type=F32,
            ).astype(BF16)
            for wy in range(2):
                cf[wx, wy, part * LENGTH : (part + 1) * LENGTH] = found[
                    :, wy * LENGTH : (wy + 1) * LENGTH
                ]

    def group_of(wx, wy):
        return group[2 * gx + wx, 2 * gy + wy]

    for wx in range(2):
        for wy in range(2):
            swept = jnp.dot(
                big[group_of(wx, wy)], cf[wx, wy], preferred_element_type=F32
            ).astype(BF16)
            for part in range(2):
                for piece in range(2):
                    at = part * LENGTH + piece * PIECE
                    swa[piece, wx, wy, part] = swept[at : at + PIECE]
                    at = at + 2 * PIECE
                    swb[piece, wy, wx, part] = swept[at : at + PIECE]
        if wx == 0:
            start_long([a_items[0][0]], 0)
    start(b_items[0])
    start_long([a_items[0][1]], 0)
    start_long(a_items[1], 1)
    start(b_items[1])

    def source(half, piece, x, y):
        if half == 0:
            if x in (0, 1):
                return swa.at[piece, x, y]
            return ra.at[piece, 0 if x < 0 else 1, y]
        if y in (0, 1):
            return swb.at[piece, y, x]
        return rb.at[piece, 0 if y < 0 else 1, x]

    def rows(chunk, start=0):
        return pl.ds(pl.multiple_of(start + chunk * CHUNK, CHUNK), CHUNK)

    def mix(half, piece, sums, get, put):
        def body(chunk, carry):
            at = rows(chunk)
            held = {}

            def value(x, y):
                if (x, y) not in held:
                    ref = source(half, piece, x, y)
                    held[x, y] = (ref[0, at, :].astype(F32), ref[1, at, :].astype(F32))
                return held[x, y]

            for (tx, ty), sources in sums:
                real, imag = get(tx, ty, at) if get is not None else (None, None)
                for sx, sy in sources:
                    place = PLACE[tx, ty, sx - tx, sy - ty]
                    w_real = weights[2 * place]
                    w_imag = weights[2 * place + 1]
                    v_real, v_imag = value(sx, sy)
                    add_real = w_real * v_real - w_imag * v_imag
                    add_imag = w_real * v_imag + w_imag * v_real
                    real = add_real if real is None else real + add_real
                    imag = add_imag if imag is None else imag + add_imag
                put(tx, ty, at, real, imag)
            return carry

        lax.fori_loop(0, PIECE // CHUNK, body, 0)

    def acc_get(half, piece):
        def get(tx, ty, at):
            return acc[half, piece, tx, ty, 0, at, :], acc[half, piece, tx, ty, 1, at, :]

        return get

    def acc_put(half, piece):
        def put(tx, ty, at, real, imag):
            acc[half, piece, tx, ty, 0, at, :] = real
            acc[half, piece, tx, ty, 1, at, :] = imag

        return put

    inner = [(x, y) for x in (0, 1) for y in (0, 1)]
    for piece in range(2):
        for half in range(2):
            mix(half, piece, [(target, inner) for target in inner], None, acc_put(half, piece))
        clear_missing(pa_items[piece])
        clear_missing(pb_items[piece])

    loaded("slow")

    def phase_rows(chunk, carry):
        at = rows(chunk)
        sinv[at, :], cosv[at, :] = sine_cosine(freq[0] * slow[at, :])
        return carry

    lax.fori_loop(0, TILE // CHUNK, phase_rows, 0)

    def pa_put(piece):
        def put(tx, ty, at, real, imag):
            side = 0 if ty < 0 else 1
            pa[piece, side, tx, 0, at, :] = real.astype(BF16)
            pa[piece, side, tx, 1, at, :] = imag.astype(BF16)

        return put

    def pb_put(piece):
        def put(tx, ty, at, real, imag):
            side = 0 if tx < 0 else 1
            pb[piece, side, ty, 0, at, :] = real.astype(BF16)
            pb[piece, side, ty, 1, at, :] = imag.astype(BF16)

        return put

    near = (-1, 0, 1)

    def sums_along_y(piece):
        arrive(a_items[piece])
        mix(
            0,
            piece,
            [((t, -1), [(t + d, 0) for d in near]) for t in (0, 1)]
            + [((t, 2), [(t + d, 1) for d in near]) for t in (0, 1)],
            None,
            pa_put(piece),
        )
        start(pa_items[piece])

    def sums_along_x(piece):
        arrive(b_items[piece])
        mix(
            1,
            piece,
            [((-1, t), [(0, t + d) for d in near]) for t in (0, 1)]
            + [((2, t), [(1, t + d) for d in near]) for t in (0, 1)],
            None,
            pb_put(piece),
        )
        start_long(pb_items[piece], 2 + piece)

    def add_along_x(piece):
        mix(
            0,
            piece,
            [((0, y), [(-1, 0), (-1, 1)]) for y in (0, 1)]
            + [((1, y), [(2, 0), (2, 1)]) for y in (0, 1)],
            acc_get(0, piece),
            acc_put(0, piece),
        )

    def add_along_y(piece):
        mix(
            1,
            piece,
            [((x, 0), [(0, -1), (1, -1)]) for x in (0, 1)]
            + [((x, 1), [(0, 2), (1, 2)]) for x in (0, 1)],
            acc_get(1, piece),
            acc_put(1, piece),
        )

    pass_on(a_items[0], 0)
    sums_along_x(0)
    pass_on(a_items[1], 1)
    sums_along_x(1)
    sums_along_y(0)
    add_along_y(0)
    add_along_y(1)
    pass_on(pb_items[0], 2)
    sums_along_y(1)
    add_along_x(0)
    pass_on(pb_items[1], 3)
    add_along_x(1)
    loaded("b1")
    loaded("b2")

    span = 2 * PIECE
    for piece in range(2):
        arrive(pa_items[piece])
        arrive(pb_items[piece])

        def join(chunk, carry, piece=piece):
            at = rows(chunk)
            below = rows(chunk, PIECE)
            for tx, ty in inner:
                for part in range(2):
                    lanes = slice(part * LENGTH, (part + 1) * LENGTH)
                    mixed[piece, tx, ty, at, lanes] = (
                        acc[0, piece, tx, ty, part, at, :]
                        + qa[piece, ty, tx, part, at, :].astype(F32)
                    ).astype(BF16)
                    mixed[piece, tx, ty, below, lanes] = (
                        acc[1, piece, tx, ty, part, at, :]
                        + qb[piece, tx, ty, part, at, :].astype(F32)
                    ).astype(BF16)
            return carry

        lax.fori_loop(0, PIECE // CHUNK, join, 0)
        for wx in range(2):
            for wy in range(2):
                spread = contract(mixed[piece, wx, wy], big[group_of(wx, wy)], 1, 1).astype(BF16)
                for part in range(2):
                    at = (2 * wx + part) * span
                    pg[piece, at : at + span, wy * LENGTH : (wy + 1) * LENGTH] = spread[
                        :, part * LENGTH : (part + 1) * LENGTH
                    ]
        across = jnp.dot(pg[piece], b1[...], preferred_element_type=F32).astype(BF16)
        for wx in range(2):
            for part in range(2):
                at = (2 * wx + part) * span
                second[wx, part, piece * span : (piece + 1) * span] = across[at : at + span]

    for part in range(2):
        for side, at in ((0, 0), (1, LENGTH - RIM)):
            rim = jnp.dot(
                b2[at : at + RIM], second[side, part], preferred_element_type=F32
            ).astype(BF16)
            ors[side, part] = rim[:, 0:TILE]
            occ[side, part] = rim[:, 384:512]
    start(corner_sums)
    start(row_sums)
    for part in range(2):
        pieces = [
            jnp.dot(b2[...], second[wx, part], preferred_element_type=F32) for wx in range(2)
        ]
        canvas[part, 0:STRIDE] = pieces[0][:STRIDE]
        canvas[part, STRIDE:LENGTH] = pieces[0][STRIDE:] + pieces[1][:OVER]
        canvas[part, LENGTH : TILE + OVER] = pieces[1][OVER:]
    own = slice(RIM, TILE + RIM)
    pick_rim = selector(OVER, 128, lambda r: r + 64)
    for part in range(2):
        rims = contract(pick_rim, canvas[part, own, 384:512].astype(BF16), 1, 1).astype(BF16)
        ocs[0, part] = rims[:RIM]
        ocs[1, part] = rims[RIM:]
    start(column_sums)
    first = selector(RIM, 128, lambda r: r)
    last = selector(RIM, 128, lambda r: r + 48)
    edges = (slice(RIM, 2 * RIM), slice(TILE, TILE + RIM))
    lane = lax.broadcasted_iota(jnp.int32, (128, 128), 0)
    to = lax.broadcasted_iota(jnp.int32, (128, 128), 1)
    first_corner = jnp.where((to < RIM) & (lane == to + 80), 1.0, 0.0).astype(BF16)
    last_corner = jnp.where((to >= 48) & (to < 64) & (lane == to + 16), 1.0, 0.0).astype(BF16)
    def finish_rows(chunk, lanes):
        at = rows(chunk)
        inside = rows(chunk, RIM)
        real = canvas[0, inside, lanes]
        imag = canvas[1, inside, lanes]
        cosine = cosv[at, lanes]
        sine = sinv[at, lanes]
        out_real[at, lanes] = (real * cosine - imag * sine).astype(BF16)
        out_imag[at, lanes] = (real * sine + imag * cosine).astype(BF16)

    middle = slice(128, 384)
    final = TILE // CHUNK - 1

    def finish_middle(chunk, carry):
        finish_rows(chunk, middle)
        return carry

    lax.fori_loop(1, final, finish_middle, 0)
    arrive(row_sums)
    for side in range(2):
        canvas[:, edges[side], 0:TILE] = canvas[:, edges[side], 0:TILE] + orr[side].astype(F32)
        finish_rows(side * final, middle)
    arrive(column_sums)
    for part in range(2):
        canvas[part, own, 0:128] = canvas[part, own, 0:128] + contract(ocr[0, part], first, 0, 0)
        canvas[part, own, 384:512] = canvas[part, own, 384:512] + contract(ocr[1, part], last, 0, 0)

    def finish_sides(chunk, carry):
        finish_rows(chunk, slice(0, 128))
        finish_rows(chunk, slice(384, TILE))
        return carry

    lax.fori_loop(1, final, finish_sides, 0)
    arrive(corner_sums)
    for side in range(2):
        for part in range(2):
            canvas[part, edges[side], 0:128] = canvas[part, edges[side], 0:128] + contract(
                occr[side, 0, part], first_corner, 1, 0
            )
            canvas[part, edges[side], 384:512] = canvas[part, edges[side], 384:512] + contract(
                occr[side, 1, part], last_corner, 1, 0
            )
        finish_sides(side * final, 0)
    for items in [row_rims, column_rims, corner_rims, row_sums, column_sums, corner_sums]:
        drain(items)
    for piece in range(2):
        for items in (a_items, b_items, pa_items, pb_items):
            drain(items[piece])
        passed(a_items[piece], piece)
        passed(pb_items[piece], 2 + piece)


def per_device(
    sizes, wavefield, slowness, frequencies, propagator, window_velocity_group, reach_list, coupling
):
    a1, b1, a2, b2 = (jnp.asarray(table) for table in tables())
    anywhere = pl.BlockSpec(memory_space=pl.ANY)
    vmem = pltpu.VMEM
    pieces = (2, 2, 2, 2, PIECE, LENGTH)
    groups, slots = propagator.shape[0], reach_list.shape[2]
    call = pl.pallas_call(
        functools.partial(kernel, sizes),
        out_shape=[jax.ShapeDtypeStruct((TILE, TILE), BF16)] * 2,
        in_specs=[anywhere, anywhere, pl.BlockSpec(memory_space=pltpu.SMEM)] + [anywhere] * 8,
        out_specs=[pl.BlockSpec(memory_space=pltpu.VMEM)] * 2,
        scratch_shapes=[
            vmem((2 * TILE, TILE), BF16),
            vmem((TILE, TILE), F32),
            vmem((groups, WIDE, WIDE), BF16),
            vmem((WIDE, WIDE), BF16),
            vmem((WIDE, WIDE), BF16),
            vmem((LENGTH, LENGTH), BF16),
            vmem((LENGTH, LENGTH), BF16),
            vmem((2, 2, RIM, WIDE), BF16),
            vmem((2, 2, RIM, WIDE), BF16),
            vmem((2, 2, RIM, TILE), BF16),
            vmem((2, 2, 2, RIM, 128), BF16),
            vmem((2 * TILE, WIDE), F32),
            vmem((2, TILE + OVER, WIDE), BF16),
            vmem((2, 2, WIDE, LENGTH), BF16),
        ]
        + [vmem(pieces, BF16)] * 8
        + [
            vmem((2, 2, 2, 2, 2, PIECE, LENGTH), F32),
            vmem((2, 2, 2, 2 * PIECE, WIDE), BF16),
            vmem((2, 8 * PIECE, WIDE), BF16),
            vmem((2, 2, LENGTH, WIDE), BF16),
            vmem((2, TILE + OVER, WIDE), F32),
            vmem((TILE, TILE), F32),
            vmem((TILE, TILE), F32),
            vmem((2, 2, RIM, TILE), BF16),
            vmem((2, 2, RIM, TILE), BF16),
            vmem((2, 2, RIM, TILE), BF16),
            vmem((2, 2, RIM, TILE), BF16),
            vmem((2, 2, RIM, 128), BF16),
            vmem((2, 2, 2, RIM, 128), BF16),
            pltpu.SMEM(window_velocity_group.shape, jnp.int32),
            pltpu.SMEM((slots, *reach_list.shape[:2]), jnp.int32),
            pltpu.SMEM((4, slots, 2, coupling.shape[1]), F32),
            pltpu.SMEM((2 * len(NEEDED),), F32),
            vmem((4, 2, 2, PIECE, LENGTH), BF16),
            pltpu.SemaphoreType.DMA((19,)),
            pltpu.SemaphoreType.DMA((32,)),
            pltpu.SemaphoreType.DMA((32,)),
            pltpu.SemaphoreType.DMA((4,)),
            pltpu.SemaphoreType.DMA((4,)),
        ],
        compiler_params=pltpu.CompilerParams(
            collective_id=0, has_side_effects=True, vmem_limit_bytes=60 * 1024 * 1024
        ),
    )
    parts = call(
        wavefield,
        slowness,
        frequencies,
        propagator,
        window_velocity_group,
        jnp.transpose(reach_list, (2, 0, 1)),
        jnp.transpose(coupling, (0, 2, 3, 1)),
        a1,
        b1,
        a2,
        b2,
    )
    return jnp.stack(parts)[:, None]


def solution(mesh):
    sizes = (mesh.shape["gx"], mesh.shape["gy"])
    return jax.shard_map(
        functools.partial(per_device, sizes),
        mesh=mesh,
        in_specs=(P(None, None, "gx", "gy"), P("gx", "gy"), P(), P(), P(), P(), P()),
        out_specs=P(None, None, "gx", "gy"),
        check_vma=False,
    )
```

```python
import functools

import jax
import jax.numpy as jnp
import numpy as np
from jax import lax
from jax.experimental import pallas as pl
from jax.experimental.pallas import tpu as pltpu
from jax.sharding import PartitionSpec as P

LENGTH = 256
OVER = 32
RIM = OVER // 2
STRIDE = LENGTH - OVER
TILE = 2 * STRIDE
WIDE = 2 * LENGTH
PIECE = LENGTH // 4
CHUNK = 16
BF16 = jnp.bfloat16
F32 = jnp.float32


def tables():
    points = np.arange(LENGTH) + 0.5
    cosines = np.sqrt(2.0 / LENGTH) * np.cos(np.pi / LENGTH * points[:, None] * points[None, :])
    cosines = cosines.astype(np.float32).astype(jnp.bfloat16).astype(np.float64)
    cells = np.arange(LENGTH)
    rising = np.sin(0.5 * np.pi * (cells + 0.5) / OVER)
    falling = np.cos(0.5 * np.pi * (cells - STRIDE + 0.5) / OVER)
    bell = np.where(cells < OVER, rising, np.where(cells >= STRIDE, falling, 1.0))
    tapered = cosines * bell[None, :]
    across = np.zeros((WIDE, WIDE))
    for window in range(2):
        for cell in range(LENGTH):
            at = window * STRIDE + cell - RIM
            if at < 0:
                at = TILE + at + RIM
            elif at >= TILE:
                at = RIM + at
            across[at, window * LENGTH : (window + 1) * LENGTH] = tapered[:, cell]

    def low(array):
        return np.ascontiguousarray(array).astype(np.float32).astype(jnp.bfloat16)

    order = np.arange(LENGTH).reshape(2, 2, PIECE).transpose(1, 0, 2).reshape(-1)
    return low(across), low(across.T), low(tapered), low(tapered.T[:, order])


NEEDED = []
for _tx in (0, 1):
    for _ty in (0, 1):
        NEEDED += [(_tx, _ty, _dx, _dy) for _dx in (-1, 0, 1) for _dy in (-1, 0, 1)]
for _t in (0, 1):
    NEEDED += [(_t, -1, _dx, 1) for _dx in (-1, 0, 1)]
    NEEDED += [(_t, 2, _dx, -1) for _dx in (-1, 0, 1)]
    NEEDED += [(-1, _t, 1, _dy) for _dy in (-1, 0, 1)]
    NEEDED += [(2, _t, -1, _dy) for _dy in (-1, 0, 1)]
PLACE = {key: index for index, key in enumerate(NEEDED)}


def contract(left, right, left_dim, right_dim):
    return lax.dot_general(
        left, right, (((left_dim,), (right_dim,)), ((), ())), preferred_element_type=F32
    )


def selector(rows, columns, target):
    row = lax.broadcasted_iota(jnp.int32, (rows, columns), 0)
    column = lax.broadcasted_iota(jnp.int32, (rows, columns), 1)
    return jnp.where(column == target(row), 1.0, 0.0).astype(BF16)


def sine_cosine(angle):
    turns = jnp.floor(angle * np.float32(2 / np.pi) + 0.5)
    rest = angle - turns * np.float32(1.5703125)
    rest = rest - turns * np.float32(4.837512969970703e-4)
    rest = rest - turns * np.float32(7.549789954891882e-8)
    square = rest * rest
    sine = np.float32(-1.9515295891e-4) * square + np.float32(8.3321608736e-3)
    sine = sine * square + np.float32(-1.6666654611e-1)
    sine = sine * square * rest + rest
    cosine = np.float32(2.443315711809948e-5) * square + np.float32(-1.388731625493765e-3)
    cosine = cosine * square + np.float32(4.166664568298827e-2)
    cosine = cosine * square * square + (1.0 - 0.5 * square)
    quarter = turns.astype(jnp.int32)
    swap = (quarter & 1) != 0
    first = jnp.where(swap, cosine, sine)
    second = jnp.where(swap, sine, cosine)
    first = jnp.where((quarter & 2) != 0, -first, first)
    second = jnp.where(((quarter + 1) & 2) != 0, -second, second)
    return first, second


SIDES = (-1, 1)


def lands(step):
    return 0 if step > 0 else 1


def leaves(step):
    return 1 if step > 0 else 0


def kernel(
    sizes,
    x_hbm,
    slow_hbm,
    freq,
    prop_hbm,
    group_hbm,
    reach_hbm,
    coup_hbm,
    a1_hbm,
    b1_hbm,
    a2_hbm,
    b2_hbm,
    out_real,
    out_imag,
    xv,
    slow,
    big,
    a1,
    b1,
    a2,
    b2,
    hs,
    hr,
    xr,
    hc,
    fp32,
    fp,
    cf,
    swa,
    swb,
    ra,
    rb,
    pa,
    pb,
    qa,
    qb,
    acc,
    mixed,
    pg,
    second,
    canvas,
    cosv,
    sinv,
    ors,
    orr,
    ocs,
    ocr,
    occ,
    occr,
    group,
    reach,
    coup,
    weights,
    held,
    local_sem,
    send_sem,
    recv_sem,
    pass_send,
    pass_recv,
    result,
    store_sem,
):
    size_x, size_y = sizes
    total_x = 2 * size_x
    total_y = 2 * size_y
    gx = lax.axis_index("gx")
    gy = lax.axis_index("gy")
    has = {
        ("gx", -1): gx > 0,
        ("gx", 1): gx < size_x - 1,
        ("gy", -1): gy > 0,
        ("gy", 1): gy < size_y - 1,
    }
    here = {"gx": gx, "gy": gy}
    ways = [{"gx": step} for step in SIDES] + [{"gy": step} for step in SIDES]
    ways += [{"gx": sx, "gy": sy} for sx in SIDES for sy in SIDES]

    def exists(way, sign=1):
        found = [has[axis, sign * step] for axis, step in way.items()]
        return found[0] if len(found) == 1 else jnp.logical_and(*found)

    def device(way):
        return {axis: here[axis] + step for axis, step in way.items()}

    half_x = size_x // 2
    relays = size_x % 2 == 0 and size_y % 4 == 0
    odd = lax.rem(gy, 2) == 1
    other = gy + 2 - 4 * lax.rem(lax.div(gy, 2), 2)
    leaving = {1: gx == half_x - 1, -1: gx == half_x}
    relayed = {step: jnp.logical_and(odd, leaving[step]) for step in SIDES}

    barrier = pltpu.get_barrier_semaphore()
    if relays:
        for step in SIDES:

            @pl.when(relayed[step])
            def _(step=step):
                for target in ({"gx": gx + step, "gy": other}, {"gy": other}):
                    pl.semaphore_signal(
                        barrier, inc=1, device_id=target, device_id_type=pl.DeviceIdType.MESH
                    )

    for way in ways:

        @pl.when(exists(way))
        def _(way=way):
            pl.semaphore_signal(
                barrier, inc=1, device_id=device(way), device_id_type=pl.DeviceIdType.MESH
            )

    base_x = jnp.clip(2 * gx - 1, 0, total_x - 4)
    copies = {
        "x0": [(x_hbm.at[0, 0], xv.at[0:TILE])],
        "x1": [(x_hbm.at[1, 0], xv.at[TILE:])],
        "a1": [(a1_hbm, a1)],
        "reach": [(reach_hbm, reach)],
        "coup": [(coup_hbm.at[pl.ds(base_x, 4)], coup)],
        "group": [(group_hbm, group)],
        "a2": [(a2_hbm, a2)],
    }
    for which in range(3):
        copies["real%d" % which] = [
            (prop_hbm.at[which, 0, 0], big.at[which, 0:LENGTH, 0:LENGTH]),
            (prop_hbm.at[which, 0, 0], big.at[which, LENGTH:WIDE, LENGTH:WIDE]),
            (prop_hbm.at[which, 0, 1], big.at[which, LENGTH:WIDE, 0:LENGTH]),
        ]
    copies["slow"] = [(slow_hbm, slow)]
    copies["b1"] = [(b1_hbm, b1)]
    copies["b2"] = [(b2_hbm, b2)]
    loads = {}
    number = 0
    for name, pairs in copies.items():
        loads[name] = []
        for source, target in pairs:
            loads[name].append(pltpu.make_async_copy(source, target, local_sem.at[number]))
            number += 1
    for batch in loads.values():
        for load in batch:
            load.start()

    def loaded(name):
        for load in loads[name]:
            load.wait()

    counter = [0]

    def message(way, source, target):
        counter[0] += 1
        return counter[0] - 1, way, source, target

    def copy_of(item):
        slot, way, source, target = item
        return pltpu.make_async_remote_copy(
            src_ref=source,
            dst_ref=target,
            send_sem=send_sem.at[slot],
            recv_sem=recv_sem.at[slot],
            device_id=device(way),
            device_id_type=pl.DeviceIdType.MESH,
        )

    def start(items):
        for item in items:

            @pl.when(exists(item[1]))
            def _(item=item):
                copy_of(item).start()

    def detour(item, place):
        slot, way, source, _ = item
        return pltpu.make_async_remote_copy(
            src_ref=source,
            dst_ref=held.at[place],
            send_sem=send_sem.at[slot],
            recv_sem=pass_recv.at[place],
            device_id={"gx": gx + way["gx"], "gy": other},
            device_id_type=pl.DeviceIdType.MESH,
        )

    def onward(item, place):
        slot, _, _, target = item
        return pltpu.make_async_remote_copy(
            src_ref=held.at[place],
            dst_ref=target,
            send_sem=pass_send.at[place],
            recv_sem=recv_sem.at[slot],
            device_id={"gy": other},
            device_id_type=pl.DeviceIdType.MESH,
        )

    def start_long(items, place):
        if not relays:
            start(items)
            return
        for item in items:
            step = item[1]["gx"]

            @pl.when(jnp.logical_and(exists(item[1]), jnp.logical_not(relayed[step])))
            def _(item=item):
                copy_of(item).start()

            @pl.when(relayed[step])
            def _(item=item):
                detour(item, place).start()

    def pass_on(items, place):
        if not relays:
            return
        for item in items:

            @pl.when(relayed[-item[1]["gx"]])
            def _(item=item):
                detour(item, place).wait_recv()
                onward(item, place).start()

    def passed(items, place):
        if not relays:
            return
        for item in items:

            @pl.when(relayed[-item[1]["gx"]])
            def _(item=item):
                onward(item, place).wait_send()

    def arrive(items):
        for item in items:

            @pl.when(exists(item[1], -1))
            def _(item=item):
                copy_of(item).wait_recv()

    def drain(items):
        for item in items:

            @pl.when(exists(item[1]))
            def _(item=item):
                copy_of(item).wait_send()

    def clear_missing(items):
        for item in items:

            @pl.when(jnp.logical_not(exists(item[1], -1)))
            def _(target=item[3]):
                target[...] = jnp.zeros(target.shape, target.dtype)

    row_rims = [
        message({"gx": -1}, x_hbm.at[:, 0, 0:RIM], xr.at[1]),
        message({"gx": 1}, x_hbm.at[:, 0, TILE - RIM : TILE], xr.at[0]),
    ]
    column_rims = [message({"gy": step}, hs.at[leaves(step)], hr.at[lands(step)]) for step in SIDES]
    corner_rims = [
        message(
            {"gx": sx, "gy": sy},
            hs.at[leaves(sy), :, :, 0:128] if sx < 0 else hs.at[leaves(sy), :, :, 384:512],
            hc.at[lands(sx), lands(sy)],
        )
        for sx in SIDES
        for sy in SIDES
    ]

    def sided(axis, piece, source, target):
        return [
            message({axis: step}, source.at[piece, leaves(step)], target.at[piece, lands(step)])
            for step in SIDES
        ]

    a_items = [sided("gx", piece, swa, ra) for piece in range(2)]
    b_items = [sided("gy", piece, swb, rb) for piece in range(2)]
    pa_items = [sided("gy", piece, pa, qa) for piece in range(2)]
    pb_items = [sided("gx", piece, pb, qb) for piece in range(2)]
    row_sums = [message({"gx": step}, ors.at[leaves(step)], orr.at[lands(step)]) for step in SIDES]
    column_sums = [message({"gy": step}, ocs.at[leaves(step)], ocr.at[lands(step)]) for step in SIDES]
    corner_sums = [
        message({"gx": sx, "gy": sy}, occ.at[leaves(sx)], occr.at[lands(sx), lands(sy)])
        for sx in SIDES
        for sy in SIDES
    ]

    pick = selector(OVER, TILE, lambda r: jnp.where(r < RIM, r, r + TILE - OVER))
    hs[:, :, :, 384:512] = jnp.zeros((2, 2, RIM, 128), BF16)
    for part in range(2):
        loaded("x%d" % part)
        rims = contract(pick, xv[part * TILE : (part + 1) * TILE], 1, 1).astype(BF16)
        hs[0, part, :, 0:TILE] = rims[:RIM]
        hs[1, part, :, 0:TILE] = rims[RIM:]
    for items in (row_rims, column_rims, corner_rims, row_sums, column_sums, corner_sums):
        clear_missing(items)
    expected = sum(exists(way).astype(jnp.int32) for way in ways)
    if relays:
        expected = expected + sum(2 * relayed[step].astype(jnp.int32) for step in SIDES)
    pl.semaphore_wait(barrier, expected)
    start(corner_rims)
    start(column_rims)
    start(row_rims)

    loaded("a1")
    fp32[...] = jnp.dot(xv[...], a1[:TILE], preferred_element_type=F32)

    loaded("reach")
    loaded("coup")
    for tx, ty in sorted({key[:2] for key in NEEDED}):
        at_x = 2 * gx + tx
        at_y = 2 * gy + ty
        near_x = jnp.clip(at_x, 0, total_x - 1)
        near_y = jnp.clip(at_y, 0, total_y - 1)
        row = near_x - base_x
        slots = [
            (reach[s, near_x, near_y], coup[row, s, 0, near_y], coup[row, s, 1, near_y])
            for s in range(reach.shape[0])
        ]
        for key, place in PLACE.items():
            if key[:2] != (tx, ty):
                continue
            window = (at_x + key[2]) * total_y + at_y + key[3]
            window = jnp.where(at_x + key[2] < 0, -2, window)
            real = jnp.float32(0.0)
            imag = jnp.float32(0.0)
            for entry, entry_real, entry_imag in slots:
                same = entry == window
                real = jnp.where(same, entry_real, real)
                imag = jnp.where(same, entry_imag, imag)
            weights[2 * place] = real
            weights[2 * place + 1] = imag
    for which in range(3):
        loaded("real%d" % which)
        big[which, 0:LENGTH, LENGTH:WIDE] = -big[which, LENGTH:WIDE, 0:LENGTH]
    loaded("a2")
    loaded("group")
    for piece in range(2):
        clear_missing(a_items[piece])
        clear_missing(b_items[piece])

    a1_rims = a1[TILE : TILE + OVER]
    arrive(column_rims)
    for part in range(2):
        rims = jnp.concatenate([hr[0, part, :, 0:TILE], hr[1, part, :, 0:TILE]], axis=0)
        fp[part, RIM : TILE + RIM] = (
            fp32[part * TILE : (part + 1) * TILE] + contract(rims, a1_rims, 0, 0)
        ).astype(BF16)
    arrive(row_rims)
    beyond = jnp.dot(xr[...].reshape(4 * RIM, TILE), a1[:TILE], preferred_element_type=F32)
    arrive(corner_rims)
    for side in range(2):
        corners = jnp.concatenate(
            [
                jnp.concatenate([hc[side, 0, part], hc[side, 1, part]], axis=0)
                for part in range(2)
            ],
            axis=1,
        )
        corners = contract(corners, a1_rims, 0, 0)
        skip = 48 if side == 0 else 0
        to = 0 if side == 0 else TILE + RIM
        for part in range(2):
            at = (2 * side + part) * RIM
            fp[part, to : to + RIM] = (
                beyond[at : at + RIM] + corners[part * 128 + skip : part * 128 + skip + RIM]
            ).astype(BF16)

    for wx in range(2):
        for part in range(2):
            found = jnp.dot(
                a2[...],
                fp[part, wx * STRIDE : wx * STRIDE + LENGTH],
                preferred_element_type=F32,
            ).astype(BF16)
            for wy in range(2):
                cf[wx, wy, part * LENGTH : (part + 1) * LENGTH] = found[
                    :, wy * LENGTH : (wy + 1) * LENGTH
                ]

    def group_of(wx, wy):
        return group[2 * gx + wx, 2 * gy + wy]

    for wx in range(2):
        for wy in range(2):
            swept = jnp.dot(
                big[group_of(wx, wy)], cf[wx, wy], preferred_element_type=F32
            ).astype(BF16)
            for part in range(2):
                for piece in range(2):
                    at = part * LENGTH + piece * PIECE
                    swa[piece, wx, wy, part] = swept[at : at + PIECE]
                    at = at + 2 * PIECE
                    swb[piece, wy, wx, part] = swept[at : at + PIECE]
        if wx == 0:
            start_long([a_items[0][0]], 0)
    start(b_items[0])
    start_long([a_items[0][1]], 0)
    start_long(a_items[1], 1)
    start(b_items[1])

    def source(half, piece, x, y):
        if half == 0:
            if x in (0, 1):
                return swa.at[piece, x, y]
            return ra.at[piece, 0 if x < 0 else 1, y]
        if y in (0, 1):
            return swb.at[piece, y, x]
        return rb.at[piece, 0 if y < 0 else 1, x]

    def rows(chunk, start=0):
        return pl.ds(pl.multiple_of(start + chunk * CHUNK, CHUNK), CHUNK)

    def mix(half, piece, sums, get, put):
        def body(chunk, carry):
            at = rows(chunk)
            held = {}

            def value(x, y):
                if (x, y) not in held:
                    ref = source(half, piece, x, y)
                    held[x, y] = (ref[0, at, :].astype(F32), ref[1, at, :].astype(F32))
                return held[x, y]

            for (tx, ty), sources in sums:
                real, imag = get(tx, ty, at) if get is not None else (None, None)
                for sx, sy in sources:
                    place = PLACE[tx, ty, sx - tx, sy - ty]
                    w_real = weights[2 * place]
                    w_imag = weights[2 * place + 1]
                    v_real, v_imag = value(sx, sy)
                    add_real = w_real * v_real - w_imag * v_imag
                    add_imag = w_real * v_imag + w_imag * v_real
                    real = add_real if real is None else real + add_real
                    imag = add_imag if imag is None else imag + add_imag
                put(tx, ty, at, real, imag)
            return carry

        lax.fori_loop(0, PIECE // CHUNK, body, 0)

    def acc_get(half, piece):
        def get(tx, ty, at):
            return acc[half, piece, tx, ty, 0, at, :], acc[half, piece, tx, ty, 1, at, :]

        return get

    def acc_put(half, piece):
        def put(tx, ty, at, real, imag):
            acc[half, piece, tx, ty, 0, at, :] = real
            acc[half, piece, tx, ty, 1, at, :] = imag

        return put

    inner = [(x, y) for x in (0, 1) for y in (0, 1)]
    for piece in range(2):
        for half in range(2):
            mix(half, piece, [(target, inner) for target in inner], None, acc_put(half, piece))
        clear_missing(pa_items[piece])
        clear_missing(pb_items[piece])

    loaded("slow")

    def phase_rows(chunk, carry):
        at = rows(chunk)
        sinv[at, :], cosv[at, :] = sine_cosine(freq[0] * slow[at, :])
        return carry

    lax.fori_loop(0, TILE // CHUNK, phase_rows, 0)

    def pa_put(piece):
        def put(tx, ty, at, real, imag):
            side = 0 if ty < 0 else 1
            pa[piece, side, tx, 0, at, :] = real.astype(BF16)
            pa[piece, side, tx, 1, at, :] = imag.astype(BF16)

        return put

    def pb_put(piece):
        def put(tx, ty, at, real, imag):
            side = 0 if tx < 0 else 1
            pb[piece, side, ty, 0, at, :] = real.astype(BF16)
            pb[piece, side, ty, 1, at, :] = imag.astype(BF16)

        return put

    near = (-1, 0, 1)

    def sums_along_y(piece):
        arrive(a_items[piece])
        mix(
            0,
            piece,
            [((t, -1), [(t + d, 0) for d in near]) for t in (0, 1)]
            + [((t, 2), [(t + d, 1) for d in near]) for t in (0, 1)],
            None,
            pa_put(piece),
        )
        start(pa_items[piece])

    def sums_along_x(piece):
        arrive(b_items[piece])
        mix(
            1,
            piece,
            [((-1, t), [(0, t + d) for d in near]) for t in (0, 1)]
            + [((2, t), [(1, t + d) for d in near]) for t in (0, 1)],
            None,
            pb_put(piece),
        )
        start_long(pb_items[piece], 2 + piece)

    def add_along_x(piece):
        mix(
            0,
            piece,
            [((0, y), [(-1, 0), (-1, 1)]) for y in (0, 1)]
            + [((1, y), [(2, 0), (2, 1)]) for y in (0, 1)],
            acc_get(0, piece),
            acc_put(0, piece),
        )

    def add_along_y(piece):
        mix(
            1,
            piece,
            [((x, 0), [(0, -1), (1, -1)]) for x in (0, 1)]
            + [((x, 1), [(0, 2), (1, 2)]) for x in (0, 1)],
            acc_get(1, piece),
            acc_put(1, piece),
        )

    pass_on(a_items[0], 0)
    sums_along_x(0)
    pass_on(a_items[1], 1)
    sums_along_x(1)
    sums_along_y(0)
    add_along_y(0)
    add_along_y(1)
    pass_on(pb_items[0], 2)
    sums_along_y(1)
    add_along_x(0)
    pass_on(pb_items[1], 3)
    add_along_x(1)
    loaded("b1")
    loaded("b2")

    span = 2 * PIECE
    for piece in range(2):
        arrive(pa_items[piece])
        arrive(pb_items[piece])

        def join(chunk, carry, piece=piece):
            at = rows(chunk)
            below = rows(chunk, PIECE)
            for tx, ty in inner:
                for part in range(2):
                    lanes = slice(part * LENGTH, (part + 1) * LENGTH)
                    mixed[piece, tx, ty, at, lanes] = (
                        acc[0, piece, tx, ty, part, at, :]
                        + qa[piece, ty, tx, part, at, :].astype(F32)
                    ).astype(BF16)
                    mixed[piece, tx, ty, below, lanes] = (
                        acc[1, piece, tx, ty, part, at, :]
                        + qb[piece, tx, ty, part, at, :].astype(F32)
                    ).astype(BF16)
            return carry

        lax.fori_loop(0, PIECE // CHUNK, join, 0)
        for wx in range(2):
            for wy in range(2):
                spread = contract(mixed[piece, wx, wy], big[group_of(wx, wy)], 1, 1).astype(BF16)
                for part in range(2):
                    at = (2 * wx + part) * span
                    pg[piece, at : at + span, wy * LENGTH : (wy + 1) * LENGTH] = spread[
                        :, part * LENGTH : (part + 1) * LENGTH
                    ]
        across = jnp.dot(pg[piece], b1[...], preferred_element_type=F32).astype(BF16)
        for wx in range(2):
            for part in range(2):
                at = (2 * wx + part) * span
                second[wx, part, piece * span : (piece + 1) * span] = across[at : at + span]

    for part in range(2):
        for side, at in ((0, 0), (1, LENGTH - RIM)):
            rim = jnp.dot(
                b2[at : at + RIM], second[side, part], preferred_element_type=F32
            ).astype(BF16)
            ors[side, part] = rim[:, 0:TILE]
            occ[side, part] = rim[:, 384:512]
    start(corner_sums)
    start(row_sums)
    for part in range(2):
        pieces = [
            jnp.dot(b2[...], second[wx, part], preferred_element_type=F32) for wx in range(2)
        ]
        canvas[part, 0:STRIDE] = pieces[0][:STRIDE]
        canvas[part, STRIDE:LENGTH] = pieces[0][STRIDE:] + pieces[1][:OVER]
        canvas[part, LENGTH : TILE + OVER] = pieces[1][OVER:]
    own = slice(RIM, TILE + RIM)
    pick_rim = selector(OVER, 128, lambda r: r + 64)
    for part in range(2):
        rims = contract(pick_rim, canvas[part, own, 384:512].astype(BF16), 1, 1).astype(BF16)
        ocs[0, part] = rims[:RIM]
        ocs[1, part] = rims[RIM:]
    start(column_sums)
    first = selector(RIM, 128, lambda r: r)
    last = selector(RIM, 128, lambda r: r + 48)
    edges = (slice(RIM, 2 * RIM), slice(TILE, TILE + RIM))
    lane = lax.broadcasted_iota(jnp.int32, (128, 128), 0)
    to = lax.broadcasted_iota(jnp.int32, (128, 128), 1)
    first_corner = jnp.where((to < RIM) & (lane == to + 80), 1.0, 0.0).astype(BF16)
    last_corner = jnp.where((to >= 48) & (to < 64) & (lane == to + 16), 1.0, 0.0).astype(BF16)
    def finish_rows(chunk, lanes):
        at = rows(chunk)
        inside = rows(chunk, RIM)
        real = canvas[0, inside, lanes]
        imag = canvas[1, inside, lanes]
        cosine = cosv[at, lanes]
        sine = sinv[at, lanes]
        result[0, at, lanes] = (real * cosine - imag * sine).astype(BF16)
        result[1, at, lanes] = (real * sine + imag * cosine).astype(BF16)

    middle = slice(128, 384)
    final = TILE // CHUNK - 1

    def finish_middle(chunk, carry):
        finish_rows(chunk, middle)
        return carry

    lax.fori_loop(1, final, finish_middle, 0)
    arrive(row_sums)
    for side in range(2):
        canvas[:, edges[side], 0:TILE] = canvas[:, edges[side], 0:TILE] + orr[side].astype(F32)
        finish_rows(side * final, middle)
    arrive(column_sums)
    for part in range(2):
        canvas[part, own, 0:128] = canvas[part, own, 0:128] + contract(ocr[0, part], first, 0, 0)
        canvas[part, own, 384:512] = canvas[part, own, 384:512] + contract(ocr[1, part], last, 0, 0)

    def finish_sides(chunk, carry):
        finish_rows(chunk, slice(0, 128))
        finish_rows(chunk, slice(384, TILE))
        return carry

    lax.fori_loop(1, final, finish_sides, 0)
    stores = []

    def store(begin, end):
        for part, target in enumerate((out_real, out_imag)):
            copy = pltpu.make_async_copy(
                result.at[part, begin:end], target.at[begin:end], store_sem.at[len(stores)]
            )
            copy.start()
            stores.append(copy)

    store(CHUNK, TILE - CHUNK)
    arrive(corner_sums)
    for side in range(2):
        for part in range(2):
            canvas[part, edges[side], 0:128] = canvas[part, edges[side], 0:128] + contract(
                occr[side, 0, part], first_corner, 1, 0
            )
            canvas[part, edges[side], 384:512] = canvas[part, edges[side], 384:512] + contract(
                occr[side, 1, part], last_corner, 1, 0
            )
        finish_sides(side * final, 0)
        store(side * final * CHUNK, side * final * CHUNK + CHUNK)
    for copy in stores:
        copy.wait()
    for items in [row_rims, column_rims, corner_rims, row_sums, column_sums, corner_sums]:
        drain(items)
    for piece in range(2):
        for items in (a_items, b_items, pa_items, pb_items):
            drain(items[piece])
        passed(a_items[piece], piece)
        passed(pb_items[piece], 2 + piece)


def per_device(
    sizes, wavefield, slowness, frequencies, propagator, window_velocity_group, reach_list, coupling
):
    a1, b1, a2, b2 = (jnp.asarray(table) for table in tables())
    anywhere = pl.BlockSpec(memory_space=pl.ANY)
    vmem = pltpu.VMEM
    pieces = (2, 2, 2, 2, PIECE, LENGTH)
    groups, slots = propagator.shape[0], reach_list.shape[2]
    call = pl.pallas_call(
        functools.partial(kernel, sizes),
        out_shape=[jax.ShapeDtypeStruct((TILE, TILE), BF16)] * 2,
        in_specs=[anywhere, anywhere, pl.BlockSpec(memory_space=pltpu.SMEM)] + [anywhere] * 8,
        out_specs=[anywhere] * 2,
        scratch_shapes=[
            vmem((2 * TILE, TILE), BF16),
            vmem((TILE, TILE), F32),
            vmem((groups, WIDE, WIDE), BF16),
            vmem((WIDE, WIDE), BF16),
            vmem((WIDE, WIDE), BF16),
            vmem((LENGTH, LENGTH), BF16),
            vmem((LENGTH, LENGTH), BF16),
            vmem((2, 2, RIM, WIDE), BF16),
            vmem((2, 2, RIM, WIDE), BF16),
            vmem((2, 2, RIM, TILE), BF16),
            vmem((2, 2, 2, RIM, 128), BF16),
            vmem((2 * TILE, WIDE), F32),
            vmem((2, TILE + OVER, WIDE), BF16),
            vmem((2, 2, WIDE, LENGTH), BF16),
        ]
        + [vmem(pieces, BF16)] * 8
        + [
            vmem((2, 2, 2, 2, 2, PIECE, LENGTH), F32),
            vmem((2, 2, 2, 2 * PIECE, WIDE), BF16),
            vmem((2, 8 * PIECE, WIDE), BF16),
            vmem((2, 2, LENGTH, WIDE), BF16),
            vmem((2, TILE + OVER, WIDE), F32),
            vmem((TILE, TILE), F32),
            vmem((TILE, TILE), F32),
            vmem((2, 2, RIM, TILE), BF16),
            vmem((2, 2, RIM, TILE), BF16),
            vmem((2, 2, RIM, TILE), BF16),
            vmem((2, 2, RIM, TILE), BF16),
            vmem((2, 2, RIM, 128), BF16),
            vmem((2, 2, 2, RIM, 128), BF16),
            pltpu.SMEM(window_velocity_group.shape, jnp.int32),
            pltpu.SMEM((slots, *reach_list.shape[:2]), jnp.int32),
            pltpu.SMEM((4, slots, 2, coupling.shape[1]), F32),
            pltpu.SMEM((2 * len(NEEDED),), F32),
            vmem((4, 2, 2, PIECE, LENGTH), BF16),
            pltpu.SemaphoreType.DMA((19,)),
            pltpu.SemaphoreType.DMA((32,)),
            pltpu.SemaphoreType.DMA((32,)),
            pltpu.SemaphoreType.DMA((4,)),
            pltpu.SemaphoreType.DMA((4,)),
            vmem((2, TILE, TILE), BF16),
            pltpu.SemaphoreType.DMA((6,)),
        ],
        compiler_params=pltpu.CompilerParams(
            collective_id=0, has_side_effects=True, vmem_limit_bytes=60 * 1024 * 1024
        ),
    )
    parts = call(
        wavefield,
        slowness,
        frequencies,
        propagator,
        window_velocity_group,
        jnp.transpose(reach_list, (2, 0, 1)),
        jnp.transpose(coupling, (0, 2, 3, 1)),
        a1,
        b1,
        a2,
        b2,
    )
    return jnp.stack(parts)[:, None]


def solution(mesh):
    sizes = (mesh.shape["gx"], mesh.shape["gy"])
    return jax.shard_map(
        functools.partial(per_device, sizes),
        mesh=mesh,
        in_specs=(P(None, None, "gx", "gy"), P("gx", "gy"), P(), P(), P(), P(), P()),
        out_specs=P(None, None, "gx", "gy"),
        check_vma=False,
    )
```
